1024 devices in a mesh: grid: 128 (over z, x, core), mem: 8 (over y).
Axes of the slice: x: 8, y: 8, z: 8, core: 2. Of those that a mesh axis runs over, the one named last changes fastest.
Arguments:
- perturb: float32 [64, 1, 1024, 256], P('mem', None, 'grid'), may hold values from -8 to 8
- winds: float32 [2, 1, 1024, 256], P(None, None, 'grid'), may hold values from -0.6 to 0.6
- kappa: float32 [1], replicated, may hold values from 0.05 to 0.2
- obs_col: int32 [1024, 256], P('grid'), may hold values from 0 to 255
- innov: float32 [1, 1024, 256], P(None, 'grid'), may hold values from -6 to 6
- alpha: float32 [64], replicated, may hold values from -5 to 5
- loc_mask: int32 [64, 1024, 8], P('mem', 'grid'), may hold values 0 or 1
Outputs:
- factor: float32 [64, 64], replicated
- newton: float32 [64], replicated
- sens: float32 [64, 1, 1024, 256], P('mem', None, 'grid')
The draws below stay inside these ranges and needn't reach their ends.
All inputs are finite; a program needn't handle non-finite values. No bound on the sum of `loc_mask` on one device may be relied on, other than what follows from the above.
Results may differ from the reference program's by a relative error of at most 0.000086.
Values sent between devices are 32-bit elements; how exact they have to be, the bound alone decides.
No kernel may reach another device: no remote copies, remote signals or barrier semaphores. Data moves between devices by JAX's collectives and lax.ppermute only.
A program may use at most 32 MiB of HBM per device.

```python
import math
import jax
import jax.numpy as jnp
from jax import lax

M = 64
L = 1
STEPS = 4
NB = 8
NX = 256
K = 256
NY = 1024
NOBS = 262144


def draw_perturb(key, part):
    rowpos = jnp.arange(NY, dtype=jnp.float32)[None, None, :, None] / max(NY - 1, 1)
    ramp = 0.5 * jnp.power(3.0, rowpos)
    key_base = jax.random.fold_in(key, 11)
    key_coef = jax.random.fold_in(key, 23)
    key_modes = jax.random.fold_in(key, 37)
    coef = jnp.clip(jax.random.normal(key_coef, (M, 8), jnp.float32), -3.0, 3.0)
    modes = jnp.clip(jax.random.normal(key_modes, (8, L, NY, NX), jnp.float32), -4.0, 4.0)
    base = jnp.clip(jax.random.normal(key_base, (M, L, NY, NX), jnp.float32), -4.0, 4.0)
    weight_common = 0.4
    common = jnp.zeros((M, L, NY, NX), jnp.float32)
    for rank_index in range(8):
        common = common + coef[:, rank_index][:, None, None, None] * modes[rank_index][None]
    return jnp.clip((base + weight_common * common) * ramp, -8.0, 8.0)


def touch_ends(entries, stream_key, smallest, high):
    longest = entries.shape.index(max(entries.shape))
    spots = []
    for shift in (0, 1):
        where = [jax.random.randint(jax.random.fold_in(stream_key, axis), (), 0, length) for axis, length in enumerate(entries.shape)]
        where[longest] = (where[longest] + shift) % entries.shape[longest]
        spots.append(tuple(where))
    return entries.at[spots[0]].set(smallest).at[spots[1]].set(high)


def level_of(key, shape, split, low, largest):
    def one(dim, shards_of):
        steps = jax.random.uniform(jax.random.fold_in(jax.random.fold_in(key, 6), dim), (shards_of,), jnp.float32, low / len(split), largest / len(split))
        return jnp.repeat(jnp.exp(steps), shape[dim] // shards_of).reshape((-1,) + (1,) * (len(shape) - dim - 1))

    loudness = one(*split[0])
    for cut in split[1:]:
        loudness = loudness * one(*cut)
    return loudness


def centred(stream_key, dims, spread, reach, pieces=(), kind=jnp.bfloat16):
    factor_of = level_of(stream_key, dims, pieces, -0.22, 0.18) if pieces else 1.0
    values = jax.random.normal(stream_key, dims, jnp.float32) * spread * factor_of
    return jnp.minimum(jnp.maximum(values, -reach), reach).astype(kind)


def setup_inputs(seed: int = 0) -> dict:
    key_list = jax.random.split(jax.random.key(seed), 8)
    perturb = draw_perturb(jax.random.fold_in(key_list[7], 71), 0)
    winds = jnp.clip(jax.random.uniform(key_list[1], (2, L, NY, NX), jnp.float32, -0.6, 0.6) * level_of(key_list[1], (2, L, NY, NX), ((2, 128),), -0.4, 0.0), -0.6, 0.6)
    kappa = jnp.clip(jnp.exp(jax.random.uniform(key_list[2], (L,), jnp.float32, math.log(0.05), math.log(0.2))), 0.05, 0.2)
    obs_col = touch_ends(jax.random.randint(key_list[3], (NY, K), 0, NX), jax.random.fold_in(key_list[3], 1), 0, NX - 1).astype(jnp.int32)
    innov = centred(key_list[4], (L, NY, K), 1.0, 6.0, ((1, 128),), jnp.float32)
    alpha = centred(key_list[5], (M,), 1.0, 5.0, (), jnp.float32)
    loc_mask = touch_ends((jax.random.randint(key_list[6], (M, NY, NB), 0, 4) < 3).astype(jnp.int32), jax.random.fold_in(key_list[6], 1), 0, 1)
    return {"perturb": perturb, "winds": winds, "kappa": kappa, "obs_col": obs_col, "innov": innov, "alpha": alpha, "loc_mask": loc_mask}


def tangent_update(field, uwind, vwind, diffusivity):
    centre = field[..., 1:-1, :]
    east = jnp.roll(centre, -1, axis=-1)
    west = jnp.roll(centre, 1, axis=-1)
    north = field[..., 2:, :]
    south = field[..., :-2, :]
    ucen = uwind[:, 1:-1, :]
    vcen = vwind[:, 1:-1, :]
    return centre - 0.5 * ucen * (east - west) - 0.5 * vcen * (north - south) + diffusivity * (east + west + north + south - 4.0 * centre)

def adjoint_update(field, uwind, vwind, diffusivity):
    centre = field[..., 1:-1, :]
    zonal = uwind[:, 1:-1, :] * centre
    merid = vwind * field
    east = jnp.roll(centre, -1, axis=-1)
    west = jnp.roll(centre, 1, axis=-1)
    lap = east + west + field[..., 2:, :] + field[..., :-2, :] - 4.0 * centre
    advect = 0.5 * (jnp.roll(zonal, -1, axis=-1) - jnp.roll(zonal, 1, axis=-1)) + 0.5 * (merid[..., 2:, :] - merid[..., :-2, :])
    return centre + advect + diffusivity * lap

def halo_rows_added(field):
    return jnp.pad(field, ((0, 0), (1, 1), (0, 0)))

def reference(perturb, winds, kappa, obs_col, innov, alpha, loc_mask):
    diffusivity = kappa[:, None, None]
    zonal_padded = halo_rows_added(winds[0])
    meridional_padded = halo_rows_added(winds[1])
    index = jnp.broadcast_to(obs_col[None], (L, NY, K))

    def forward(member):
        model_state = member
        for step in range(STEPS):
            model_state = tangent_update(halo_rows_added(model_state), zonal_padded, meridional_padded, diffusivity)
        return jnp.take_along_axis(model_state, index, axis=2)
    hy = lax.map(forward, perturb)
    scale = 1.0 / M ** 0.5
    resid = innov - jnp.einsum('m,mlyk->lyk', alpha, hy, precision=lax.Precision.HIGHEST) * scale
    flat = hy.reshape(M, -1)
    gram = jnp.dot(flat, flat.T, precision=lax.Precision.HIGHEST)
    proj = jnp.dot(flat, resid.reshape(-1), precision=lax.Precision.HIGHEST)
    count = float(NOBS)
    hess = jnp.eye(M, dtype=jnp.float32) + gram / count
    grad = alpha - M ** 0.5 * proj / count
    lower = jnp.linalg.cholesky(hess)
    factor = lower.T
    newton = jax.scipy.linalg.cho_solve((lower, True), grad)
    levels = jnp.arange(L, dtype=jnp.int32)[:, None, None]
    rowsidx = jnp.arange(NY, dtype=jnp.int32)[None, :, None]
    forcing = jnp.zeros((L, NY, NX), jnp.float32).at[levels, rowsidx, index].add(resid)
    maskf = jnp.repeat(loc_mask.astype(jnp.float32), NX // NB, axis=2)

    def backward(maskrow):
        model_state = maskrow[None] * forcing
        for step in range(STEPS):
            model_state = adjoint_update(halo_rows_added(model_state), zonal_padded, meridional_padded, diffusivity)
        return model_state
    sens = lax.map(backward, maskf)
    return (factor, newton, sens)
```

```python
import functools

import jax
import jax.numpy as jnp
from jax import lax
from jax.experimental import pallas as pl
from jax.experimental.pallas import tpu as pltpu
from jax.sharding import Mesh
from jax.sharding import PartitionSpec as P

STEPS = 4
F32 = jnp.float32
HI = lax.Precision.HIGHEST
GRID = ("z", "x", "core")
PACK = 24


def vmem():
    return pl.BlockSpec(memory_space=pltpu.VMEM)


def call(body, outs, *args, flops=1_000_000):
    moved = sum(a.size * 4 for a in args) + sum(o.size * 4 for o in outs)
    return pl.pallas_call(
        body,
        out_shape=outs,
        in_specs=[vmem() for _ in args],
        out_specs=[vmem() for _ in outs],
        cost_estimate=pl.CostEstimate(flops=flops, bytes_accessed=moved, transcendentals=0),
        compiler_params=pltpu.CompilerParams(vmem_limit_bytes=8 * 2**20),
        name=body.__name__,
    )(*args)


def shape(*dims):
    return jax.ShapeDtypeStruct(dims, F32)


def pack_halo(field, winds, up, down):
    rows = jnp.swapaxes(field[...], 0, 1)
    down[0:4] = rows[0:4]
    up[0:4] = rows[4:8]
    down[4, 0:4, :] = winds[0:4, :]
    down[4, 4:8, :] = winds[8:12, :]
    up[4, 0:4, :] = winds[4:8, :]
    up[4, 4:8, :] = winds[12:16, :]
    down[5] = jnp.ones((8, 256), F32)
    up[5] = jnp.ones((8, 256), F32)


def bin_observations(col, innov, mask, binned, spread):
    slots = lax.broadcasted_iota(jnp.int32, (256, 256), 0)
    hit = (slots == col[...]).astype(F32)
    row = lax.broadcasted_iota(jnp.int32, (8, 256), 0)
    values = jnp.where(row == 0, 1.0, jnp.broadcast_to(innov[...], (8, 256)))
    binned[...] = lax.dot_general(
        values, hit, (((1,), (1,)), ((), ())), precision=HI, preferred_element_type=F32
    )
    block = lax.broadcasted_iota(jnp.int32, (8, 256), 1) // 32
    expand = (block == lax.broadcasted_iota(jnp.int32, (8, 256), 0)).astype(F32)
    wide = jnp.dot(mask[...].astype(F32), expand, preferred_element_type=F32)
    spread[...] = jnp.swapaxes(wide.reshape(8, 8, 256), 0, 1)


def east(x):
    return pltpu.roll(x, 255, 1)


def west(x):
    return pltpu.roll(x, 1, 1)


def wind_rows(blocks, r):
    tile = blocks[r // 4]
    u = jnp.broadcast_to(tile[4, r % 4 : r % 4 + 1, :], (8, 256))
    v = jnp.broadcast_to(tile[4, 4 + r % 4 : 5 + r % 4, :], (8, 256))
    return 0.5 * u, 0.5 * v


def tangent(low, down, up, high, kappa, out):
    blocks = (low, down, up, high)
    k = jnp.broadcast_to(kappa[...], (8, 256))
    winds = [wind_rows(blocks, r) for r in range(16)]
    rows = [blocks[r // 4][r % 4] for r in range(16)]
    for step in range(1, STEPS + 1):
        new = list(rows)
        for r in range(step, 16 - step):
            hu, hv = winds[r]
            c = rows[r]
            value = (
                (1.0 - 4.0 * k) * c
                + (k - hu) * east(c)
                + (k + hu) * west(c)
                + (k - hv) * rows[r + 1]
                + (k + hv) * rows[r - 1]
            )
            if r < 4:
                value = value * low[5]
            if r > 11:
                value = value * high[5]
            new[r] = value
        rows = new
    for y in range(8):
        out[y] = rows[4 + y]


def adjoint(low, down, up, high, plow, pdown, pup, phigh, kappa, out):
    blocks = (low, down, up, high)
    states = (plow, pdown, pup, phigh)
    k = jnp.broadcast_to(kappa[...], (8, 256))
    winds = [wind_rows(blocks, r) for r in range(16)]
    rows = [states[r // 4][r % 4] for r in range(16)]
    for step in range(1, STEPS + 1):
        new = list(rows)
        for r in range(step, 16 - step):
            hu, _ = winds[r]
            c = rows[r]
            value = (
                (1.0 - 4.0 * k) * c
                + east((k + hu) * c)
                + west((k - hu) * c)
                + (k + winds[r + 1][1]) * rows[r + 1]
                + (k - winds[r - 1][1]) * rows[r - 1]
            )
            if r < 4:
                value = value * low[5]
            if r > 11:
                value = value * high[5]
            new[r] = value
        rows = new
    out[...] = jnp.swapaxes(jnp.stack(rows[4:12], axis=0), 0, 1)


def iota2(dims, axis):
    return lax.broadcasted_iota(jnp.int32, dims, axis)


def gram_block(field, binned, alpha, out):
    copies = out.shape[0]
    x = field[...]
    count = binned[0:1, :]
    weighted = jnp.sum(alpha[...] * x, axis=0, keepdims=True) * 0.125
    forcing = binned[1:2, :] - count * weighted
    left = jnp.concatenate([x * count, jnp.broadcast_to(forcing, (8, 256))], axis=0)
    right = jnp.concatenate([x, x], axis=0)
    g = lax.dot_general(
        left, right, (((1,), (1,)), ((), ())), precision=HI, preferred_element_type=F32
    )
    lane = iota2((16, 128), 1)
    first = lane < 64
    i = iota2((16, 128), 0) + jnp.where(first, 0, 16)
    j = lane % 64
    shifted = pltpu.roll(g[32:64], 96, 1)
    top = jnp.where(first, g[0:16], g[16:32])
    low = jnp.where(first, shifted[0:16], shifted[16:32])
    packed = jnp.where((j < 32) & (i > j), low, top)
    on_diagonal = iota2((32, 128), 1) == iota2((32, 128), 0) + 96
    diagonal = jnp.sum(jnp.where(on_diagonal, g[32:64], 0.0), axis=0, keepdims=True)
    sub = iota2((8, 128), 0)
    extra = jnp.where(iota2((8, 128), 1) < 64, g[64:72], diagonal)
    tail = jnp.where(
        sub == 0,
        extra,
        jnp.where(sub == 1, forcing[:, :128], jnp.where(sub == 2, forcing[:, 128:], 0.0)),
    )
    for c in range(copies):
        out[c, 0:16, :] = packed
        out[c, 16:24, :] = tail


def sum_blocks(parts):
    total = parts[0]
    for c in range(1, parts.shape[0]):
        total = total + parts[c]
    return total


def first_sum(parts, spread, core, out, pdown, pup):
    rows = parts.shape[0] // 2
    total = parts[0:PACK, :]
    for c in range(1, parts.shape[0] // PACK):
        total = total + parts[PACK * c : PACK * c + PACK, :]
    for c in range(out.shape[0]):
        out[c] = total
    odd = core[...] > 0.5
    halves = []
    for h in range(2):
        a = parts[pl.ds(17 + h, 8, stride=PACK), :]
        b = parts[pl.ds(17 + h + rows, 8, stride=PACK), :]
        halves.append(jnp.where(odd, b, a))
    forcing = jnp.concatenate(halves, axis=1)
    for y in range(8):
        value = spread[y] * forcing[y : y + 1, :]
        if y < 4:
            pdown[y] = value
        else:
            pup[y - 4] = value


def next_sum(parts, out):
    total = sum_blocks(parts)
    for c in range(out.shape[0]):
        out[c] = total


def newton_step(count, parts, alpha, factor, newton):
    total = sum_blocks(parts)
    packed, extra = total[0:16], total[16:17]
    lane, sub = iota2((32, 128), 1), iota2((32, 128), 0)
    s = jnp.concatenate([packed, pltpu.roll(packed, 64, 1)], axis=0)
    top = jnp.where((lane >= sub) & (lane < 64), s, 0.0)
    diagonal = pltpu.roll(jnp.broadcast_to(extra, (32, 128)), 64, 1)
    bottom = jnp.where(
        lane == sub + 32,
        diagonal,
        jnp.where((lane >= 32) & (lane < sub + 32), pltpu.roll(s, 32, 1), 0.0),
    )
    z = jnp.concatenate([top, bottom, jnp.zeros((64, 128), F32)], axis=0)
    lanes, subs = iota2((64, 128), 1), iota2((64, 128), 0)
    both = z[0:64] + jnp.where(lanes == subs, 0.0, jnp.transpose(z)[0:64])
    scale = 1.0 / count
    a = jnp.where(lanes == subs, 1.0, 0.0) + both * scale
    a = jnp.where(lanes == subs + 64, 1.0, a)
    tiles = [a[8 * t : 8 * t + 8] for t in range(8)]
    sub8 = iota2((8, 128), 0)
    for k in range(64):
        t, q = divmod(k, 8)
        row = jnp.broadcast_to(tiles[t][q : q + 1, :], (8, 128))
        pivot = jnp.broadcast_to(row[:, k : k + 1], (8, 128))
        scaled = row / pivot
        for i in range(t, 8):
            mult = jnp.broadcast_to(tiles[i][:, k : k + 1], (8, 128))
            if i == t:
                mult = jnp.where(sub8 > q, mult, 0.0)
            tiles[i] = tiles[i] - mult * scaled
    u = jnp.concatenate(tiles, axis=0)
    d = jnp.sum(jnp.where(lanes == subs, u, 0.0), axis=1, keepdims=True)
    upper = jnp.where((lanes >= subs) & (lanes < 64), u, 0.0) / jnp.sqrt(d)
    factor[...] = upper[:, 0:64]
    rhs = alpha[...] - 8.0 * extra * scale
    rhs = jnp.where(iota2((1, 128), 1) < 64, rhs, 0.0)
    inverse = jnp.where(lanes >= 64, u, 0.0)
    y = jnp.sum(inverse * pltpu.roll(rhs, 64, 1), axis=1, keepdims=True) / d
    x = jnp.sum(inverse * y, axis=0, keepdims=True)
    newton[...] = pltpu.roll(x, 64, 1)[:, 0:64]


def per_device(perturb, winds, kappa, obs_col, innov, alpha, loc_mask):
    ny = lax.axis_size("y")
    blocks = lax.axis_size(GRID)
    count = float(blocks * 8 * 256)
    up, down = call(
        pack_halo,
        [shape(6, 8, 256)] * 2,
        perturb.reshape(8, 8, 256),
        winds.reshape(16, 256),
    )
    forward = [(i, i + 1) for i in range(blocks - 1)]
    backward = [(i + 1, i) for i in range(blocks - 1)]
    low = lax.ppermute(up, GRID, forward)
    high = lax.ppermute(down, GRID, backward)
    mine = lax.axis_index("y")
    core = lax.axis_index("core").astype(F32).reshape(1, 1)
    k = kappa.reshape(1, 1)
    binned, spread = call(
        bin_observations,
        [shape(8, 256), shape(8, 8, 256)],
        lax.dynamic_slice_in_dim(obs_col, mine, 1, 0),
        lax.dynamic_slice_in_dim(innov[0], mine, 1, 0),
        loc_mask.reshape(64, 8),
    )
    (evolved,) = call(tangent, [shape(8, 8, 256)], low, down, up, high, k)
    field = lax.all_to_all(evolved, "y", 0, 0, tiled=True).reshape(64, 256)
    (part,) = call(
        gram_block, [shape(2 * ny, PACK, 128)], field, binned, alpha.reshape(64, 1)
    )
    parts = lax.all_to_all(part, ("core", "y"), 0, 0, tiled=True)
    part, pdown, pup = call(
        first_sum,
        [shape(lax.axis_size("x"), PACK, 128), shape(4, 8, 256), shape(4, 8, 256)],
        parts.reshape(-1, 128),
        spread,
        core,
    )
    parts = lax.all_to_all(part, "x", 0, 0, tiled=True)
    plow = lax.ppermute(pup, GRID, forward)
    phigh = lax.ppermute(pdown, GRID, backward)
    (part,) = call(next_sum, [shape(lax.axis_size("z"), PACK, 128)], parts)
    parts = lax.all_to_all(part, "z", 0, 0, tiled=True)
    (sens,) = call(
        adjoint, [shape(8, 8, 256)], low, down, up, high, plow, pdown, pup, phigh, k
    )
    wide = jnp.concatenate([alpha, jnp.zeros((64,), F32)]).reshape(1, 128)
    final = functools.partial(newton_step, count)
    final.__name__ = "newton_step"
    factor, newton = call(final, [shape(64, 64), shape(1, 64)], parts, wide)
    return factor, newton.reshape(64), sens.reshape(8, 1, 8, 256)


def solution(mesh):
    grid, mem = mesh.devices.shape
    side = int((grid // 2) ** 0.5)
    fine = Mesh(mesh.devices.reshape(side, grid // 2 // side, 2, mem), GRID + ("y",))
    in_specs = (
        P("y", None, GRID, None),
        P(None, None, GRID, None),
        P(),
        P(GRID, None),
        P(None, GRID, None),
        P(),
        P("y", GRID, None),
    )
    out_specs = (P(), P(), P("y", None, GRID, None))
    return jax.shard_map(
        per_device, mesh=fine, in_specs=in_specs, out_specs=out_specs, check_vma=False
    )
```

```python
import functools

import jax
import jax.numpy as jnp
from jax import lax
from jax.experimental import pallas as pl
from jax.experimental.pallas import tpu as pltpu
from jax.sharding import Mesh
from jax.sharding import PartitionSpec as P

STEPS = 4
F32 = jnp.float32
HI = lax.Precision.HIGHEST
GRID = ("z", "x", "core")
PACK = 24


def vmem():
    return pl.BlockSpec(memory_space=pltpu.VMEM)


def call(body, outs, *args, flops=1_000_000, space=pltpu.VMEM, scratch=()):
    moved = sum(a.size * 4 for a in args) + sum(o.size * 4 for o in outs)
    return pl.pallas_call(
        body,
        out_shape=outs,
        in_specs=[pl.BlockSpec(memory_space=space) for _ in args],
        out_specs=[vmem() for _ in outs],
        scratch_shapes=scratch,
        cost_estimate=pl.CostEstimate(flops=flops, bytes_accessed=moved, transcendentals=0),
        compiler_params=pltpu.CompilerParams(vmem_limit_bytes=8 * 2**20),
        name=body.__name__,
    )(*args)


def shape(*dims):
    return jax.ShapeDtypeStruct(dims, F32)


def iota2(dims, axis):
    return lax.broadcasted_iota(jnp.int32, dims, axis)


def pack_block(field, winds, col, innov, mask, out, *scratch):
    held, sems = scratch[:5], scratch[5]
    copies = [
        pltpu.make_async_copy(source, target, sems.at[n])
        for n, (source, target) in enumerate(zip((field, winds, col, innov, mask), held))
    ]
    for copy in copies:
        copy.start()
    for copy in copies:
        copy.wait()
    out[0:8] = jnp.swapaxes(held[0][...], 0, 1)
    out[8] = held[1][0:8, :]
    out[9] = held[1][8:16, :]
    out[10] = held[2][...].astype(F32)
    out[11] = held[3][...]
    out[12] = jnp.ones((8, 256), F32)
    for m in range(8):
        out[12, :, 8 * m : 8 * m + 8] = held[4][m].astype(F32)


def bin_observations(low, own, high, mine, binned, spread):
    sub = iota2((8, 256), 0)
    chosen = sub == mine[...]
    hits, rows = iota2((256, 256), 0).astype(F32), []
    for kind in range(2):
        picked = []
        for tile in (10, 11):
            if kind == 0:
                source = own[tile]
            else:
                source = jnp.where(
                    sub < 4, pltpu.roll(low[tile], 4, 0), pltpu.roll(high[tile], 4, 0)
                )
            picked.append(jnp.sum(jnp.where(chosen, source, 0.0), axis=0, keepdims=True))
        hit = (hits == picked[0]).astype(F32)
        values = jnp.where(sub == 0, 1.0, jnp.broadcast_to(picked[1], (8, 256)))
        rows.append(
            lax.dot_general(
                values, hit, (((1,), (1,)), ((), ())), precision=HI, preferred_element_type=F32
            )
        )
    binned[...] = jnp.where(sub < 2, rows[0], pltpu.roll(rows[1], 2, 0))
    masks = jnp.concatenate([b[12][:, 0:128] for b in (low, own, high)], axis=0)
    wide = []
    for m in range(8):
        expand = (iota2((128, 256), 0) == 8 * m + iota2((128, 256), 1) // 32).astype(F32)
        wide.append(jnp.dot(masks, expand, preferred_element_type=F32))
    for block in range(4):
        part = jnp.stack([w[8 * (block // 2 + block % 2) : 8 * (block // 2 + block % 2) + 8] for w in wide])
        turned = jnp.swapaxes(part, 0, 1)
        if block == 0:
            spread[0:4] = turned[4:8]
        elif block == 1:
            spread[4:12] = turned
        elif block == 3:
            spread[12:16] = turned[0:4]


def east(x):
    return pltpu.roll(x, 255, 1)


def west(x):
    return pltpu.roll(x, 1, 1)


def wind_rows(blocks, r):
    u = jnp.broadcast_to(blocks[r // 8][8, r % 8 : r % 8 + 1, :], (8, 256))
    v = jnp.broadcast_to(blocks[r // 8][9, r % 8 : r % 8 + 1, :], (8, 256))
    return 0.5 * u, 0.5 * v


def inside(block):
    flag = block[12][:, 128:256]
    return jnp.concatenate([flag, flag], axis=1)


def tangent(low, own, high, kappa, out):
    blocks = (low, own, high)
    k = jnp.broadcast_to(kappa[...], (8, 256))
    below, above = inside(low), inside(high)
    rows = [blocks[r // 8][r % 8] for r in range(24)]
    winds = [wind_rows(blocks, r) for r in range(24)]
    for step in range(1, STEPS + 1):
        new = list(rows)
        for r in range(step, 24 - step):
            hu, hv = winds[r]
            c = rows[r]
            value = (
                (1.0 - 4.0 * k) * c
                + (k - hu) * east(c)
                + (k + hu) * west(c)
                + (k - hv) * rows[r + 1]
                + (k + hv) * rows[r - 1]
            )
            if r < 8:
                value = value * below
            if r > 15:
                value = value * above
            new[r] = value
        rows = new
    for y in range(8):
        out[y, 0] = rows[8 + y]
        out[y, 1] = rows[4 + y] if y < 4 else rows[12 + y]


def adjoint(low, own, high, state, kappa, out):
    blocks = (low, own, high)
    k = jnp.broadcast_to(kappa[...], (8, 256))
    below, above = inside(low), inside(high)
    rows = {4 + e: state[e] for e in range(16)}
    winds = {r: wind_rows(blocks, r) for r in range(4, 20)}
    for step in range(1, STEPS + 1):
        new = dict(rows)
        for r in range(4 + step, 20 - step):
            hu, _ = winds[r]
            c = rows[r]
            value = (
                (1.0 - 4.0 * k) * c
                + east((k + hu) * c)
                + west((k - hu) * c)
                + (k + winds[r + 1][1]) * rows[r + 1]
                + (k - winds[r - 1][1]) * rows[r - 1]
            )
            if r < 8:
                value = value * below
            if r > 15:
                value = value * above
            new[r] = value
        rows = new
    out[...] = jnp.swapaxes(jnp.stack([rows[8 + y] for y in range(8)], axis=0), 0, 1)


def gram_block(field, binned, alpha, out):
    copies = out.shape[0]
    x = field[:, 0].reshape(64, 256)
    ghost = field[:, 1].reshape(64, 256)
    count = binned[0:1, :]
    weighted = jnp.sum(alpha[...] * x, axis=0, keepdims=True) * 0.125
    forcing = binned[1:2, :] - count * weighted
    beyond = jnp.sum(alpha[...] * ghost, axis=0, keepdims=True) * 0.125
    beyond = binned[3:4, :] - binned[2:3, :] * beyond
    left = jnp.concatenate([x * count, jnp.broadcast_to(forcing, (8, 256))], axis=0)
    right = jnp.concatenate([x, x], axis=0)
    g = lax.dot_general(
        left, right, (((1,), (1,)), ((), ())), precision=HI, preferred_element_type=F32
    )
    lane = iota2((16, 128), 1)
    first = lane < 64
    i = iota2((16, 128), 0) + jnp.where(first, 0, 16)
    j = lane % 64
    shifted = pltpu.roll(g[32:64], 96, 1)
    top = jnp.where(first, g[0:16], g[16:32])
    low = jnp.where(first, shifted[0:16], shifted[16:32])
    packed = jnp.where((j < 32) & (i > j), low, top)
    on_diagonal = iota2((32, 128), 1) == iota2((32, 128), 0) + 96
    diagonal = jnp.sum(jnp.where(on_diagonal, g[32:64], 0.0), axis=0, keepdims=True)
    sub = iota2((8, 128), 0)
    extra = jnp.where(iota2((8, 128), 1) < 64, g[64:72], diagonal)
    tail = extra
    for n, line in enumerate((forcing, beyond)):
        for h in range(2):
            tail = jnp.where(sub == 2 * n + h + 1, line[:, 128 * h : 128 * h + 128], tail)
    for c in range(copies):
        out[c, 0:16, :] = packed
        out[c, 16:24, :] = tail


def sum_blocks(parts):
    total = parts[0]
    for c in range(1, parts.shape[0]):
        total = total + parts[c]
    return total


def first_sum(parts, spread, core, out, state):
    rows = parts.shape[0] // 2
    total = parts[0:PACK, :]
    for c in range(1, parts.shape[0] // PACK):
        total = total + parts[PACK * c : PACK * c + PACK, :]
    for c in range(out.shape[0]):
        out[c] = total
    odd = core[...] > 0.5
    forcing = []
    for n in range(2):
        halves = []
        for h in range(2):
            a = parts[pl.ds(17 + 2 * n + h, 8, stride=PACK), :]
            b = parts[pl.ds(17 + 2 * n + h + rows, 8, stride=PACK), :]
            halves.append(jnp.where(odd, b, a))
        forcing.append(jnp.concatenate(halves, axis=1))
    for e in range(16):
        if e < 4:
            line = forcing[1][e : e + 1, :]
        elif e < 12:
            line = forcing[0][e - 4 : e - 3, :]
        else:
            line = forcing[1][e - 8 : e - 7, :]
        state[e] = spread[e] * line


def next_sum(parts, out):
    total = sum_blocks(parts)
    for c in range(out.shape[0]):
        out[c] = total


def across(tile, lane):
    return jnp.broadcast_to(tile[:, lane : lane + 1], tile.shape)


def along(tile, row):
    return jnp.broadcast_to(tile[row : row + 1, :], tile.shape)


def newton_step(count, parts, alpha, factor, newton):
    total = sum_blocks(parts)
    packed, extra = total[0:16], total[16:17]
    lane, sub = iota2((32, 128), 1), iota2((32, 128), 0)
    s = jnp.concatenate([packed, pltpu.roll(packed, 64, 1)], axis=0)
    top = jnp.where((lane >= sub) & (lane < 64), s, 0.0)
    diagonal = pltpu.roll(jnp.broadcast_to(extra, (32, 128)), 64, 1)
    bottom = jnp.where(
        lane == sub + 32,
        diagonal,
        jnp.where((lane >= 32) & (lane < sub + 32), pltpu.roll(s, 32, 1), 0.0),
    )
    scale = 1.0 / count
    rhs = alpha[...] - 8.0 * extra * scale
    rest = jnp.where(iota2((64, 128), 0) == 0, jnp.broadcast_to(rhs, (64, 128)), 0.0)
    z = jnp.concatenate([top, bottom, rest], axis=0)
    turned = jnp.transpose(z)[0:64]
    lanes, subs = iota2((64, 128), 1), iota2((64, 128), 0)
    both = z[0:64] + jnp.where((lanes == subs) | (lanes >= 64), 0.0, turned)
    a = jnp.where((lanes == subs) | (lanes == subs + 64), 1.0, 0.0) + both * scale
    tiles = [a[8 * t : 8 * t + 8] for t in range(8)]
    right = [across(turned[8 * t : 8 * t + 8], 64) for t in range(8)]
    lane1 = iota2((1, 128), 1)
    solved = jnp.zeros((8, 128), F32)
    for t in range(8):
        base = 8 * t
        columns = [across(tiles[t], base + c) for c in range(8)]
        e = {(i, c): along(columns[c], i) for c in range(8) for i in range(c, 8)}
        line = [along(tiles[t], q) for q in range(8)]
        b = [along(right[t], q) for q in range(8)]
        low, inverse = {}, []
        for c in range(8):
            inverse.append(1.0 / e[c, c])
            for i in range(c + 1, 8):
                low[i, c] = e[i, c] * inverse[c]
            for j in range(c + 1, 8):
                for i in range(j, 8):
                    e[i, j] = e[i, j] - low[i, c] * e[j, c]
            for i in range(c + 1, 8):
                line[i] = line[i] - low[i, c] * line[c]
                b[i] = b[i] - low[i, c] * b[c]
        for i in range(t + 1, 8):
            c_of = []
            for c in range(8):
                value = across(tiles[i], base + c)
                for j in range(c):
                    value = value - c_of[j] * low[c, j]
                c_of.append(value)
            for c in range(8):
                mult = c_of[c] * inverse[c]
                tiles[i] = tiles[i] - mult * line[c]
                right[i] = right[i] - mult * b[c]
        for q in range(8):
            solved = solved + line[q] * (b[q] * inverse[q])
            upper = line[q][0:1] * lax.rsqrt(e[q, q][0:1])
            upper = jnp.where(lane1 >= base + q, upper, 0.0)
            factor[base + q : base + q + 1, :] = upper[:, 0:64]
    newton[...] = pltpu.roll(solved, 64, 1)[0:1, 0:64]


def per_device(perturb, winds, kappa, obs_col, innov, alpha, loc_mask):
    ny = lax.axis_size("y")
    blocks = lax.axis_size(GRID)
    count = float(blocks * 8 * 256)
    sources = (
        perturb.reshape(8, 8, 256),
        winds.reshape(16, 256),
        obs_col,
        innov.reshape(8, 256),
        loc_mask,
    )
    (own,) = call(
        pack_block,
        [shape(13, 8, 256)],
        *(pltpu.with_memory_space_constraint(a, pltpu.HBM) for a in sources),
        space=pltpu.HBM,
        scratch=[pltpu.VMEM(a.shape, a.dtype) for a in sources]
        + [pltpu.SemaphoreType.DMA((len(sources),))],
    )
    low = lax.ppermute(own, GRID, [(i, i + 1) for i in range(blocks - 1)])
    high = lax.ppermute(own, GRID, [(i + 1, i) for i in range(blocks - 1)])
    core = lax.axis_index("core").astype(F32).reshape(1, 1)
    k = kappa.reshape(1, 1)
    (evolved,) = call(tangent, [shape(8, 2, 8, 256)], low, own, high, k)
    binned, spread = call(
        bin_observations,
        [shape(8, 256), shape(16, 8, 256)],
        low,
        own,
        high,
        lax.axis_index("y").reshape(1, 1),
    )
    field = lax.all_to_all(evolved, "y", 0, 0, tiled=True)
    (part,) = call(
        gram_block, [shape(2 * ny, PACK, 128)], field, binned, alpha.reshape(64, 1)
    )
    parts = lax.all_to_all(part, ("core", "y"), 0, 0, tiled=True)
    part, state = call(
        first_sum,
        [shape(lax.axis_size("x"), PACK, 128), shape(16, 8, 256)],
        parts.reshape(-1, 128),
        spread,
        core,
    )
    parts = lax.all_to_all(part, "x", 0, 0, tiled=True)
    (part,) = call(next_sum, [shape(lax.axis_size("z"), PACK, 128)], parts)
    parts = lax.all_to_all(part, "z", 0, 0, tiled=True)
    (sens,) = call(adjoint, [shape(8, 8, 256)], low, own, high, state, k)
    wide = jnp.concatenate([alpha, jnp.zeros((64,), F32)]).reshape(1, 128)
    final = functools.partial(newton_step, count)
    final.__name__ = "newton_step"
    factor, newton = call(final, [shape(64, 64), shape(1, 64)], parts, wide)
    return factor, newton.reshape(64), sens.reshape(8, 1, 8, 256)


def solution(mesh):
    grid, mem = mesh.devices.shape
    side = int((grid // 2) ** 0.5)
    fine = Mesh(mesh.devices.reshape(side, grid // 2 // side, 2, mem), GRID + ("y",))
    in_specs = (
        P("y", None, GRID, None),
        P(None, None, GRID, None),
        P(),
        P(GRID, None),
        P(None, GRID, None),
        P(),
        P("y", GRID, None),
    )
    out_specs = (P(), P(), P("y", None, GRID, None))
    return jax.shard_map(
        per_device, mesh=fine, in_specs=in_specs, out_specs=out_specs, check_vma=False
    )
```

```python
import functools

import jax
import jax.numpy as jnp
from jax import lax
from jax.experimental import pallas as pl
from jax.experimental.pallas import tpu as pltpu
from jax.sharding import Mesh
from jax.sharding import PartitionSpec as P

STEPS = 4
F32 = jnp.float32
HI = lax.Precision.HIGHEST
GRID = ("z", "x", "core")
PACK = 24


def vmem():
    return pl.BlockSpec(memory_space=pltpu.VMEM)


def call(body, outs, *args, flops=1_000_000, space=pltpu.VMEM, scratch=()):
    moved = sum(a.size * 4 for a in args) + sum(o.size * 4 for o in outs)
    return pl.pallas_call(
        body,
        out_shape=outs,
        in_specs=[pl.BlockSpec(memory_space=space) for _ in args],
        out_specs=[vmem() for _ in outs],
        scratch_shapes=scratch,
        cost_estimate=pl.CostEstimate(flops=flops, bytes_accessed=moved, transcendentals=0),
        compiler_params=pltpu.CompilerParams(vmem_limit_bytes=8 * 2**20),
        name=body.__name__,
    )(*args)


def shape(*dims):
    return jax.ShapeDtypeStruct(dims, F32)


def iota2(dims, axis):
    return lax.broadcasted_iota(jnp.int32, dims, axis)


def pack_block(field, winds, col, innov, mask, out, *scratch):
    held, sems = scratch[:5], scratch[5]
    copies = [
        pltpu.make_async_copy(source, target, sems.at[n])
        for n, (source, target) in enumerate(zip((field, winds, col, innov, mask), held))
    ]
    for copy in copies:
        copy.start()
    for copy in copies:
        copy.wait()
    out[0:8] = jnp.swapaxes(held[0][...], 0, 1)
    out[8] = held[1][0:8, :]
    out[9] = held[1][8:16, :]
    out[10] = held[2][...].astype(F32)
    out[11] = held[3][...]
    out[12] = jnp.zeros((8, 256), F32)
    for m in range(8):
        out[12, :, 8 * m : 8 * m + 8] = held[4][m].astype(F32)


def east(x):
    return pltpu.roll(x, 255, 1)


def west(x):
    return pltpu.roll(x, 1, 1)


def wind_rows(blocks, r):
    u = jnp.broadcast_to(blocks[r // 8][8, r % 8 : r % 8 + 1, :], (8, 256))
    v = jnp.broadcast_to(blocks[r // 8][9, r % 8 : r % 8 + 1, :], (8, 256))
    return 0.5 * u, 0.5 * v


def select_row(tile, sub, mine):
    return jnp.sum(jnp.where(sub == mine, tile, 0.0), axis=0, keepdims=True)


def tangent(low, own, kappa, mine, joined, alpha, core, follows, out, binned, column_of):
    column_of[...] = jnp.transpose(jnp.broadcast_to(alpha[...], (128, 128)))[0:64]
    blocks = (low, own)
    k = jnp.broadcast_to(kappa[...], (8, 256))
    joint = jnp.broadcast_to(joined[...], (8, 256))
    rows = [blocks[r // 8][r % 8] for r in range(16)]
    winds = [wind_rows(blocks, r) for r in range(16)]
    for step in range(1, STEPS + 1):
        new = list(rows)
        for r in range(step, 16 - step):
            hu, hv = winds[r]
            c = rows[r]
            north = (k - hv) * rows[r + 1]
            south = (k + hv) * rows[r - 1]
            if r == 7:
                north = north * joint
            if r == 8:
                south = south * joint
            new[r] = (
                (1.0 - 4.0 * k) * c + (k - hu) * east(c) + (k + hu) * west(c) + north + south
            )
        rows = new
    for y in range(8):
        out[y] = rows[4 + y]
    sub = iota2((8, 256), 0)
    turned = [
        jnp.where(sub < 4, pltpu.roll(low[tile], 4, 0), pltpu.roll(own[tile], 4, 0))
        for tile in (10, 11)
    ]
    column, value = (select_row(tile, sub, mine[...]) for tile in turned)
    hit = (iota2((256, 256), 0).astype(F32) == column).astype(F32)
    values = jnp.where(sub == 0, 1.0, jnp.broadcast_to(value, (8, 256)))
    binned[...] = lax.dot_general(
        values, hit, (((1,), (1,)), ((), ())), precision=HI, preferred_element_type=F32
    )


def adjoint(low, own, window, beyond, kappa, joined, follows, out):
    k = jnp.broadcast_to(kappa[...], (8, 256))
    below = jnp.broadcast_to(joined[...], (8, 256))
    above = jnp.broadcast_to(follows[...], (8, 256))
    masks = jnp.concatenate([b[:, 0:128] for b in (low[12], own[12], beyond[3])], axis=0)
    wide = []
    for m in range(8):
        expand = (iota2((128, 256), 0) == 8 * m + iota2((128, 256), 1) // 32).astype(F32)
        wide.append(jnp.dot(masks, expand, preferred_element_type=F32))
    spread = [
        jnp.swapaxes(jnp.stack([w[8 * n : 8 * n + 8] for w in wide]), 0, 1) for n in range(3)
    ]
    rows, winds = {}, {}
    for e in range(16):
        line = window[0, e : e + 1, :] if e < 8 else beyond[0, e - 8 : e - 7, :]
        n, y = divmod(e + 4, 8)
        rows[e] = spread[n][y] * line
        if e < 4:
            rows[e] = rows[e] * below
        if e > 11:
            rows[e] = rows[e] * above
        u, v = ((low[8], low[9]), (own[8], own[9]), (beyond[1], beyond[2]))[n]
        winds[e] = tuple(0.5 * jnp.broadcast_to(w[y : y + 1], (8, 256)) for w in (u, v))
    for step in range(1, STEPS + 1):
        new = dict(rows)
        for r in range(step, 16 - step):
            hu, _ = winds[r]
            c = rows[r]
            value = (
                (1.0 - 4.0 * k) * c
                + east((k + hu) * c)
                + west((k - hu) * c)
                + (k + winds[r + 1][1]) * rows[r + 1]
                + (k - winds[r - 1][1]) * rows[r - 1]
            )
            if r < 4:
                value = value * below
            if r > 11:
                value = value * above
            new[r] = value
        rows = new
    out[...] = jnp.swapaxes(jnp.stack([rows[4 + y] for y in range(8)], axis=0), 0, 1)


def gram_block(field, binned, alpha, out):
    copies = out.shape[0]
    x = field[...].reshape(64, 256)
    count = binned[0:1, :]
    weights = jnp.concatenate([alpha[...], alpha[...]], axis=1)
    weighted = jnp.sum(weights * x, axis=0, keepdims=True) * 0.125
    forcing = binned[1:2, :] - count * weighted
    left = jnp.concatenate([x * count, jnp.broadcast_to(forcing, (8, 256))], axis=0)
    right = jnp.concatenate([x, x], axis=0)
    g = lax.dot_general(
        left, right, (((1,), (1,)), ((), ())), precision=HI, preferred_element_type=F32
    )
    lane = iota2((16, 128), 1)
    first = lane < 64
    i = iota2((16, 128), 0) + jnp.where(first, 0, 16)
    j = lane % 64
    shifted = pltpu.roll(g[32:64], 96, 1)
    top = jnp.where(first, g[0:16], g[16:32])
    low = jnp.where(first, shifted[0:16], shifted[16:32])
    packed = jnp.where((j < 32) & (i > j), low, top)
    on_diagonal = iota2((32, 128), 1) == iota2((32, 128), 0) + 96
    diagonal = jnp.sum(jnp.where(on_diagonal, g[32:64], 0.0), axis=0, keepdims=True)
    sub = iota2((8, 128), 0)
    extra = jnp.where(iota2((8, 128), 1) < 64, g[64:72], diagonal)
    tail = extra
    for h in range(2):
        tail = jnp.where(sub == h + 1, forcing[:, 128 * h : 128 * h + 128], tail)
    for c in range(copies):
        out[c, 0:16, :] = packed
        out[c, 16:24, :] = tail


def sum_blocks(parts):
    total = parts[0]
    for c in range(1, parts.shape[0]):
        total = total + parts[c]
    return total


def first_sum(parts, own, core, out, window):
    rows = parts.shape[0] // 2
    total = parts[0:PACK, :]
    for c in range(1, parts.shape[0] // PACK):
        total = total + parts[PACK * c : PACK * c + PACK, :]
    for c in range(out.shape[0]):
        out[c] = total
    odd = core[...] > 0.5
    for h in range(2):
        a = parts[pl.ds(17 + h, 8, stride=PACK), :]
        b = parts[pl.ds(17 + h + rows, 8, stride=PACK), :]
        window[0, :, 128 * h : 128 * h + 128] = jnp.where(odd, b, a)
    window[1] = own[8]
    window[2] = own[9]
    window[3] = own[12]


def next_sum(parts, out):
    total = sum_blocks(parts)
    for c in range(out.shape[0]):
        out[c] = total


def across(tile, lane):
    return jnp.broadcast_to(tile[:, lane : lane + 1], tile.shape)


def along(tile, row):
    return jnp.broadcast_to(tile[row : row + 1, :], tile.shape)


def newton_step(count, parts, alpha, factor, newton):
    total = sum_blocks(parts)
    packed, extra = total[0:16], total[16:17]
    lane, sub = iota2((32, 128), 1), iota2((32, 128), 0)
    s = jnp.concatenate([packed, pltpu.roll(packed, 64, 1)], axis=0)
    top = jnp.where((lane >= sub) & (lane < 64), s, 0.0)
    diagonal = pltpu.roll(jnp.broadcast_to(extra, (32, 128)), 64, 1)
    bottom = jnp.where(
        lane == sub + 32,
        diagonal,
        jnp.where((lane >= 32) & (lane < sub + 32), pltpu.roll(s, 32, 1), 0.0),
    )
    scale = 1.0 / count
    rhs = alpha[...] - 8.0 * extra * scale
    rest = jnp.where(iota2((64, 128), 0) == 0, jnp.broadcast_to(rhs, (64, 128)), 0.0)
    z = jnp.concatenate([top, bottom, rest], axis=0)
    turned = jnp.transpose(z)[0:64]
    lanes, subs = iota2((64, 128), 1), iota2((64, 128), 0)
    both = z[0:64] + jnp.where((lanes == subs) | (lanes >= 64), 0.0, turned)
    a = jnp.where((lanes == subs) | (lanes == subs + 64), 1.0, 0.0) + both * scale
    tiles = [a[8 * t : 8 * t + 8] for t in range(8)]
    right = [across(turned[8 * t : 8 * t + 8], 64) for t in range(8)]
    lane1 = iota2((1, 128), 1)
    solved = jnp.zeros((8, 128), F32)
    for t in range(8):
        base = 8 * t
        columns = [across(tiles[t], base + c) for c in range(8)]
        e = {(i, c): along(columns[c], i) for c in range(8) for i in range(c, 8)}
        line = [along(tiles[t], q) for q in range(8)]
        b = [along(right[t], q) for q in range(8)]
        low, inverse = {}, []
        for c in range(8):
            inverse.append(1.0 / e[c, c])
            for i in range(c + 1, 8):
                low[i, c] = e[i, c] * inverse[c]
            for j in range(c + 1, 8):
                for i in range(j, 8):
                    e[i, j] = e[i, j] - low[i, c] * e[j, c]
            for i in range(c + 1, 8):
                line[i] = line[i] - low[i, c] * line[c]
                b[i] = b[i] - low[i, c] * b[c]
        for i in range(t + 1, 8):
            c_of = []
            for c in range(8):
                value = across(tiles[i], base + c)
                for j in range(c):
                    value = value - c_of[j] * low[c, j]
                c_of.append(value)
            for c in range(8):
                mult = c_of[c] * inverse[c]
                tiles[i] = tiles[i] - mult * line[c]
                right[i] = right[i] - mult * b[c]
        for q in range(8):
            solved = solved + line[q] * (b[q] * inverse[q])
            upper = line[q][0:1] * lax.rsqrt(e[q, q][0:1])
            upper = jnp.where(lane1 >= base + q, upper, 0.0)
            factor[base + q : base + q + 1, :] = upper[:, 0:64]
    newton[...] = pltpu.roll(solved, 64, 1)[0:1, 0:64]


def per_device(perturb, winds, kappa, obs_col, innov, alpha, loc_mask):
    ny = lax.axis_size("y")
    blocks = lax.axis_size(GRID)
    count = float(blocks * 8 * 256)
    sources = (
        perturb.reshape(8, 8, 256),
        winds.reshape(16, 256),
        obs_col,
        innov.reshape(8, 256),
        loc_mask,
    )
    (own,) = call(
        pack_block,
        [shape(13, 8, 256)],
        *(pltpu.with_memory_space_constraint(a, pltpu.HBM) for a in sources),
        space=pltpu.HBM,
        scratch=[pltpu.VMEM(a.shape, a.dtype) for a in sources]
        + [pltpu.SemaphoreType.DMA((len(sources),))],
    )
    low = lax.ppermute(own, GRID, [(i, (i + 1) % blocks) for i in range(blocks)])
    index = lax.axis_index(GRID)
    core = lax.axis_index("core").astype(F32).reshape(1, 1)
    joined = (index > 0).astype(F32).reshape(1, 1)
    follows = (index < blocks - 1).astype(F32).reshape(1, 1)
    mine = lax.axis_index("y").reshape(1, 1)
    k = kappa.reshape(1, 1)
    wide = jnp.concatenate([alpha, jnp.zeros((64,), F32)]).reshape(1, 128)
    evolved, binned, column = call(
        tangent,
        [shape(8, 8, 256), shape(8, 256), shape(64, 128)],
        low,
        own,
        k,
        mine,
        joined,
        wide,
        core,
        follows,
    )
    field = lax.all_to_all(evolved, "y", 0, 0, tiled=True)
    (part,) = call(gram_block, [shape(2 * ny, PACK, 128)], field, binned, column)
    parts = lax.all_to_all(part, ("core", "y"), 0, 0, tiled=True)
    part, window = call(
        first_sum,
        [shape(lax.axis_size("x"), PACK, 128), shape(4, 8, 256)],
        parts.reshape(-1, 128),
        own,
        core,
    )
    parts = lax.all_to_all(part, "x", 0, 0, tiled=True)
    (part,) = call(next_sum, [shape(lax.axis_size("z"), PACK, 128)], parts)
    parts = lax.all_to_all(part, "z", 0, 0, tiled=True)
    beyond = lax.ppermute(window, GRID, [((i + 1) % blocks, i) for i in range(blocks)])
    (sens,) = call(
        adjoint, [shape(8, 8, 256)], low, own, window, beyond, k, joined, follows
    )
    final = functools.partial(newton_step, count)
    final.__name__ = "newton_step"
    factor, newton = call(final, [shape(64, 64), shape(1, 64)], parts, wide)
    return factor, newton.reshape(64), sens.reshape(8, 1, 8, 256)


def solution(mesh):
    grid, mem = mesh.devices.shape
    side = int((grid // 2) ** 0.5)
    fine = Mesh(mesh.devices.reshape(side, grid // 2 // side, 2, mem), GRID + ("y",))
    in_specs = (
        P("y", None, GRID, None),
        P(None, None, GRID, None),
        P(),
        P(GRID, None),
        P(None, GRID, None),
        P(),
        P("y", GRID, None),
    )
    out_specs = (P(), P(), P("y", None, GRID, None))
    return jax.shard_map(
        per_device, mesh=fine, in_specs=in_specs, out_specs=out_specs, check_vma=False
    )
```

```python
import functools

import jax
import jax.numpy as jnp
from jax import lax
from jax.experimental import pallas as pl
from jax.experimental.pallas import tpu as pltpu
from jax.sharding import Mesh
from jax.sharding import PartitionSpec as P

STEPS = 4
F32 = jnp.float32
HI = lax.Precision.HIGHEST
GRID = ("z", "x", "core")
CORE = 17 * 128
PACK = CORE + 256


def vmem():
    return pl.BlockSpec(memory_space=pltpu.VMEM)


def call(body, outs, *args, flops=1_000_000, space=pltpu.VMEM, scratch=()):
    moved = sum(a.size * 4 for a in args) + sum(o.size * 4 for o in outs)
    return pl.pallas_call(
        body,
        out_shape=outs,
        in_specs=[pl.BlockSpec(memory_space=space) for _ in args],
        out_specs=[vmem() for _ in outs],
        scratch_shapes=scratch,
        cost_estimate=pl.CostEstimate(flops=flops, bytes_accessed=moved, transcendentals=0),
        compiler_params=pltpu.CompilerParams(vmem_limit_bytes=8 * 2**20),
        name=body.__name__,
    )(*args)


def shape(*dims):
    return jax.ShapeDtypeStruct(dims, F32)


def iota2(dims, axis):
    return lax.broadcasted_iota(jnp.int32, dims, axis)


def pack_block(field, winds, col, innov, mask, out, *scratch):
    held, sems = scratch[:5], scratch[5]
    copies = [
        pltpu.make_async_copy(source, target, sems.at[n])
        for n, (source, target) in enumerate(zip((field, winds, col, innov, mask), held))
    ]
    for copy in copies:
        copy.start()
    for copy in copies:
        copy.wait()
    out[0:8] = jnp.swapaxes(held[0][...], 0, 1)
    out[8] = held[1][0:8, :]
    out[9] = held[1][8:16, :]
    out[10] = held[2][...].astype(F32)
    out[11] = held[3][...]
    out[12] = jnp.zeros((8, 256), F32)
    for m in range(8):
        out[12, :, 8 * m : 8 * m + 8] = held[4][m].astype(F32)


def east(x):
    return pltpu.roll(x, 255, 1)


def west(x):
    return pltpu.roll(x, 1, 1)


def wind_rows(blocks, r):
    u = jnp.broadcast_to(blocks[r // 8][8, r % 8 : r % 8 + 1, :], (8, 256))
    v = jnp.broadcast_to(blocks[r // 8][9, r % 8 : r % 8 + 1, :], (8, 256))
    return 0.5 * u, 0.5 * v


def select_row(tile, sub, mine):
    return jnp.sum(jnp.where(sub == mine, tile, 0.0), axis=0, keepdims=True)


def tangent(low, own, kappa, mine, joined, alpha, core, follows, out, binned, column_of):
    column_of[...] = jnp.transpose(jnp.broadcast_to(alpha[...], (128, 128)))[0:64]
    blocks = (low, own)
    k = jnp.broadcast_to(kappa[...], (8, 256))
    joint = jnp.broadcast_to(joined[...], (8, 256))
    rows = [blocks[r // 8][r % 8] for r in range(16)]
    winds = [wind_rows(blocks, r) for r in range(16)]
    for step in range(1, STEPS + 1):
        new = list(rows)
        for r in range(step, 16 - step):
            hu, hv = winds[r]
            c = rows[r]
            north = (k - hv) * rows[r + 1]
            south = (k + hv) * rows[r - 1]
            if r == 7:
                north = north * joint
            if r == 8:
                south = south * joint
            new[r] = (
                (1.0 - 4.0 * k) * c + (k - hu) * east(c) + (k + hu) * west(c) + north + south
            )
        rows = new
    for y in range(8):
        out[y] = rows[4 + y]
    sub = iota2((8, 256), 0)
    turned = [
        jnp.where(sub < 4, pltpu.roll(low[tile], 4, 0), pltpu.roll(own[tile], 4, 0))
        for tile in (10, 11)
    ]
    column, value = (select_row(tile, sub, mine[...]) for tile in turned)
    hit = (iota2((256, 256), 0).astype(F32) == column).astype(F32)
    values = jnp.where(sub == 0, 1.0, jnp.broadcast_to(value, (8, 256)))
    binned[...] = lax.dot_general(
        values, hit, (((1,), (1,)), ((), ())), precision=HI, preferred_element_type=F32
    )


def adjoint(low, own, window, beyond, kappa, joined, follows, out):
    k = jnp.broadcast_to(kappa[...], (8, 256))
    below = jnp.broadcast_to(joined[...], (8, 256))
    above = jnp.broadcast_to(follows[...], (8, 256))
    masks = jnp.concatenate([b[:, 0:128] for b in (low[12], own[12], beyond[3])], axis=0)
    wide = []
    for m in range(8):
        expand = (iota2((128, 256), 0) == 8 * m + iota2((128, 256), 1) // 32).astype(F32)
        wide.append(jnp.dot(masks, expand, preferred_element_type=F32))
    spread = [
        jnp.swapaxes(jnp.stack([w[8 * n : 8 * n + 8] for w in wide]), 0, 1) for n in range(3)
    ]
    rows, winds = {}, {}
    for e in range(16):
        line = window[0, e : e + 1, :] if e < 8 else beyond[0, e - 8 : e - 7, :]
        n, y = divmod(e + 4, 8)
        rows[e] = spread[n][y] * line
        if e < 4:
            rows[e] = rows[e] * below
        if e > 11:
            rows[e] = rows[e] * above
        u, v = ((low[8], low[9]), (own[8], own[9]), (beyond[1], beyond[2]))[n]
        winds[e] = tuple(0.5 * jnp.broadcast_to(w[y : y + 1], (8, 256)) for w in (u, v))
    for step in range(1, STEPS + 1):
        new = dict(rows)
        for r in range(step, 16 - step):
            hu, _ = winds[r]
            c = rows[r]
            value = (
                (1.0 - 4.0 * k) * c
                + east((k + hu) * c)
                + west((k - hu) * c)
                + (k + winds[r + 1][1]) * rows[r + 1]
                + (k - winds[r - 1][1]) * rows[r - 1]
            )
            if r < 4:
                value = value * below
            if r > 11:
                value = value * above
            new[r] = value
        rows = new
    out[...] = jnp.swapaxes(jnp.stack([rows[4 + y] for y in range(8)], axis=0), 0, 1)


def gram_block(field, binned, alpha, out):
    copies = out.shape[0]
    x = field[...].reshape(64, 256)
    count = binned[0:1, :]
    weights = jnp.concatenate([alpha[...], alpha[...]], axis=1)
    weighted = jnp.sum(weights * x, axis=0, keepdims=True) * 0.125
    forcing = binned[1:2, :] - count * weighted
    left = jnp.concatenate([x * count, jnp.broadcast_to(forcing, (8, 256))], axis=0)
    right = jnp.concatenate([x, x], axis=0)
    g = lax.dot_general(
        left, right, (((1,), (1,)), ((), ())), precision=HI, preferred_element_type=F32
    )
    lane = iota2((16, 128), 1)
    first = lane < 64
    i = iota2((16, 128), 0) + jnp.where(first, 0, 16)
    j = lane % 64
    shifted = pltpu.roll(g[32:64], 96, 1)
    top = jnp.where(first, g[0:16], g[16:32])
    low = jnp.where(first, shifted[0:16], shifted[16:32])
    packed = jnp.where((j < 32) & (i > j), low, top)
    on_diagonal = iota2((32, 128), 1) == iota2((32, 128), 0) + 96
    diagonal = jnp.sum(jnp.where(on_diagonal, g[32:64], 0.0), axis=0, keepdims=True)
    extra = jnp.where(iota2((1, 128), 1) < 64, g[64:65], diagonal)
    flat = jnp.concatenate([packed[r : r + 1] for r in range(16)] + [extra, forcing], axis=1)
    for c in range(copies):
        out[c] = flat


def sum_blocks(parts):
    total = parts[0]
    for c in range(1, parts.shape[0]):
        total = total + parts[c]
    return total


def first_sum(parts, own, core, out, window):
    half = parts.shape[0] // 2
    total = sum_blocks(parts)[:, 0:CORE]
    for c in range(out.shape[0]):
        out[c] = total
    odd = core[...] > 0.5
    for y in range(8):
        window[0, y : y + 1, :] = jnp.where(
            odd, parts[half + y][:, CORE:PACK], parts[y][:, CORE:PACK]
        )
    window[1] = own[8]
    window[2] = own[9]
    window[3] = own[12]


def next_sum(parts, out):
    total = sum_blocks(parts)
    for c in range(out.shape[0]):
        out[c] = total


def across(tile, lane):
    return jnp.broadcast_to(tile[:, lane : lane + 1], tile.shape)


def along(tile, row):
    return jnp.broadcast_to(tile[row : row + 1, :], tile.shape)


def newton_step(count, parts, alpha, factor, newton):
    total = sum_blocks(parts)
    packed = jnp.concatenate([total[:, 128 * r : 128 * r + 128] for r in range(16)], axis=0)
    extra = total[:, CORE - 128 : CORE]
    lane, sub = iota2((32, 128), 1), iota2((32, 128), 0)
    s = jnp.concatenate([packed, pltpu.roll(packed, 64, 1)], axis=0)
    top = jnp.where((lane >= sub) & (lane < 64), s, 0.0)
    diagonal = pltpu.roll(jnp.broadcast_to(extra, (32, 128)), 64, 1)
    bottom = jnp.where(
        lane == sub + 32,
        diagonal,
        jnp.where((lane >= 32) & (lane < sub + 32), pltpu.roll(s, 32, 1), 0.0),
    )
    scale = 1.0 / count
    rhs = alpha[...] - 8.0 * extra * scale
    rest = jnp.where(iota2((64, 128), 0) == 0, jnp.broadcast_to(rhs, (64, 128)), 0.0)
    z = jnp.concatenate([top, bottom, rest], axis=0)
    turned = jnp.transpose(z)[0:64]
    lanes, subs = iota2((64, 128), 1), iota2((64, 128), 0)
    both = z[0:64] + jnp.where((lanes == subs) | (lanes >= 64), 0.0, turned)
    a = jnp.where((lanes == subs) | (lanes == subs + 64), 1.0, 0.0) + both * scale
    tiles = [a[8 * t : 8 * t + 8] for t in range(8)]
    right = [across(turned[8 * t : 8 * t + 8], 64) for t in range(8)]
    lane1 = iota2((1, 128), 1)
    solved = jnp.zeros((8, 128), F32)
    for t in range(8):
        base = 8 * t
        columns = [across(tiles[t], base + c) for c in range(8)]
        e = {(i, c): along(columns[c], i) for c in range(8) for i in range(c, 8)}
        line = [along(tiles[t], q) for q in range(8)]
        b = [along(right[t], q) for q in range(8)]
        low, inverse = {}, []
        for c in range(8):
            inverse.append(1.0 / e[c, c])
            for i in range(c + 1, 8):
                low[i, c] = e[i, c] * inverse[c]
            for j in range(c + 1, 8):
                for i in range(j, 8):
                    e[i, j] = e[i, j] - low[i, c] * e[j, c]
            for i in range(c + 1, 8):
                line[i] = line[i] - low[i, c] * line[c]
                b[i] = b[i] - low[i, c] * b[c]
        for i in range(t + 1, 8):
            c_of = []
            for c in range(8):
                value = across(tiles[i], base + c)
                for j in range(c):
                    value = value - c_of[j] * low[c, j]
                c_of.append(value)
            for c in range(8):
                mult = c_of[c] * inverse[c]
                tiles[i] = tiles[i] - mult * line[c]
                right[i] = right[i] - mult * b[c]
        for q in range(8):
            solved = solved + line[q] * (b[q] * inverse[q])
            upper = line[q][0:1] * lax.rsqrt(e[q, q][0:1])
            upper = jnp.where(lane1 >= base + q, upper, 0.0)
            factor[base + q : base + q + 1, :] = upper[:, 0:64]
    newton[...] = pltpu.roll(solved, 64, 1)[0:1, 0:64]


def per_device(perturb, winds, kappa, obs_col, innov, alpha, loc_mask):
    ny = lax.axis_size("y")
    blocks = lax.axis_size(GRID)
    count = float(blocks * 8 * 256)
    sources = (
        perturb.reshape(8, 8, 256),
        winds.reshape(16, 256),
        obs_col,
        innov.reshape(8, 256),
        loc_mask,
    )
    (own,) = call(
        pack_block,
        [shape(13, 8, 256)],
        *(pltpu.with_memory_space_constraint(a, pltpu.HBM) for a in sources),
        space=pltpu.HBM,
        scratch=[pltpu.VMEM(a.shape, a.dtype) for a in sources]
        + [pltpu.SemaphoreType.DMA((len(sources),))],
    )
    low = lax.ppermute(own, GRID, [(i, (i + 1) % blocks) for i in range(blocks)])
    index = lax.axis_index(GRID)
    core = lax.axis_index("core").astype(F32).reshape(1, 1)
    joined = (index > 0).astype(F32).reshape(1, 1)
    follows = (index < blocks - 1).astype(F32).reshape(1, 1)
    mine = lax.axis_index("y").reshape(1, 1)
    k = kappa.reshape(1, 1)
    wide = jnp.concatenate([alpha, jnp.zeros((64,), F32)]).reshape(1, 128)
    evolved, binned, column = call(
        tangent,
        [shape(8, 8, 256), shape(8, 256), shape(64, 128)],
        low,
        own,
        k,
        mine,
        joined,
        wide,
        core,
        follows,
    )
    field = lax.all_to_all(evolved, "y", 0, 0, tiled=True)
    (part,) = call(gram_block, [shape(2 * ny, 1, PACK)], field, binned, column)
    parts = lax.all_to_all(part, ("core", "y"), 0, 0, tiled=True)
    part, window = call(
        first_sum,
        [shape(lax.axis_size("x"), 1, CORE), shape(4, 8, 256)],
        parts,
        own,
        core,
    )
    parts = lax.all_to_all(part, "x", 0, 0, tiled=True)
    (part,) = call(next_sum, [shape(lax.axis_size("z"), 1, CORE)], parts)
    parts = lax.all_to_all(part, "z", 0, 0, tiled=True)
    beyond = lax.ppermute(window, GRID, [((i + 1) % blocks, i) for i in range(blocks)])
    (sens,) = call(
        adjoint, [shape(8, 8, 256)], low, own, window, beyond, k, joined, follows
    )
    final = functools.partial(newton_step, count)
    final.__name__ = "newton_step"
    factor, newton = call(final, [shape(64, 64), shape(1, 64)], parts, wide)
    return factor, newton.reshape(64), sens.reshape(8, 1, 8, 256)


def solution(mesh):
    grid, mem = mesh.devices.shape
    side = int((grid // 2) ** 0.5)
    fine = Mesh(mesh.devices.reshape(side, grid // 2 // side, 2, mem), GRID + ("y",))
    in_specs = (
        P("y", None, GRID, None),
        P(None, None, GRID, None),
        P(),
        P(GRID, None),
        P(None, GRID, None),
        P(),
        P("y", GRID, None),
    )
    out_specs = (P(), P(), P("y", None, GRID, None))
    return jax.shard_map(
        per_device, mesh=fine, in_specs=in_specs, out_specs=out_specs, check_vma=False
    )
```

```python
import functools

import jax
import jax.numpy as jnp
from jax import lax
from jax.experimental import pallas as pl
from jax.experimental.pallas import tpu as pltpu
from jax.sharding import Mesh
from jax.sharding import PartitionSpec as P

STEPS = 4
F32 = jnp.float32
HI = lax.Precision.HIGHEST
GRID = ("z", "x", "core")
CORE = 17 * 128
HALF = 9 * 128
PACK = HALF + 256


def vmem():
    return pl.BlockSpec(memory_space=pltpu.VMEM)


def call(body, outs, *args, flops=1_000_000, space=pltpu.VMEM, scratch=()):
    moved = sum(a.size * 4 for a in args) + sum(o.size * 4 for o in outs)
    return pl.pallas_call(
        body,
        out_shape=outs,
        in_specs=[pl.BlockSpec(memory_space=space) for _ in args],
        out_specs=[vmem() for _ in outs],
        scratch_shapes=scratch,
        cost_estimate=pl.CostEstimate(flops=flops, bytes_accessed=moved, transcendentals=0),
        compiler_params=pltpu.CompilerParams(vmem_limit_bytes=8 * 2**20),
        name=body.__name__,
    )(*args)


def shape(*dims):
    return jax.ShapeDtypeStruct(dims, F32)


def iota2(dims, axis):
    return lax.broadcasted_iota(jnp.int32, dims, axis)


def pack_block(field, winds, col, innov, mask, out, *scratch):
    held, sems = scratch[:5], scratch[5]
    copies = [
        pltpu.make_async_copy(source, target, sems.at[n])
        for n, (source, target) in enumerate(zip((field, winds, col, innov, mask), held))
    ]
    for copy in copies:
        copy.start()
    for copy in copies:
        copy.wait()
    out[0:8] = jnp.swapaxes(held[0][...], 0, 1)
    out[8] = held[1][0:8, :]
    out[9] = held[1][8:16, :]
    out[10] = held[2][...].astype(F32)
    out[11] = held[3][...]
    out[12] = jnp.zeros((8, 256), F32)
    for m in range(8):
        out[12, :, 8 * m : 8 * m + 8] = held[4][m].astype(F32)


def east(x):
    return pltpu.roll(x, 255, 1)


def west(x):
    return pltpu.roll(x, 1, 1)


def wind_rows(blocks, r):
    u = jnp.broadcast_to(blocks[r // 8][8, r % 8 : r % 8 + 1, :], (8, 256))
    v = jnp.broadcast_to(blocks[r // 8][9, r % 8 : r % 8 + 1, :], (8, 256))
    return 0.5 * u, 0.5 * v


def select_row(tile, sub, mine):
    return jnp.sum(jnp.where(sub == mine, tile, 0.0), axis=0, keepdims=True)


def tangent(low, own, kappa, mine, joined, alpha, core, follows, out, binned, column_of):
    column_of[...] = jnp.transpose(jnp.broadcast_to(alpha[...], (128, 128)))[0:64]
    blocks = (low, own)
    k = jnp.broadcast_to(kappa[...], (8, 256))
    joint = jnp.broadcast_to(joined[...], (8, 256))
    rows = [blocks[r // 8][r % 8] for r in range(16)]
    winds = [wind_rows(blocks, r) for r in range(16)]
    for step in range(1, STEPS + 1):
        new = list(rows)
        for r in range(step, 16 - step):
            hu, hv = winds[r]
            c = rows[r]
            north = (k - hv) * rows[r + 1]
            south = (k + hv) * rows[r - 1]
            if r == 7:
                north = north * joint
            if r == 8:
                south = south * joint
            new[r] = (
                (1.0 - 4.0 * k) * c + (k - hu) * east(c) + (k + hu) * west(c) + north + south
            )
        rows = new
    for y in range(8):
        out[y] = rows[4 + y]
    sub = iota2((8, 256), 0)
    turned = [
        jnp.where(sub < 4, pltpu.roll(low[tile], 4, 0), pltpu.roll(own[tile], 4, 0))
        for tile in (10, 11)
    ]
    column, value = (select_row(tile, sub, mine[...]) for tile in turned)
    hit = (iota2((256, 256), 0).astype(F32) == column).astype(F32)
    values = jnp.where(sub == 0, 1.0, jnp.broadcast_to(value, (8, 256)))
    binned[...] = lax.dot_general(
        values, hit, (((1,), (1,)), ((), ())), precision=HI, preferred_element_type=F32
    )


def adjoint(low, own, window, beyond, kappa, joined, follows, out):
    k = jnp.broadcast_to(kappa[...], (8, 256))
    below = jnp.broadcast_to(joined[...], (8, 256))
    above = jnp.broadcast_to(follows[...], (8, 256))
    masks = jnp.concatenate([b[:, 0:128] for b in (low[12], own[12], beyond[3])], axis=0)
    wide = []
    for m in range(8):
        expand = (iota2((128, 256), 0) == 8 * m + iota2((128, 256), 1) // 32).astype(F32)
        wide.append(jnp.dot(masks, expand, preferred_element_type=F32))
    spread = [
        jnp.swapaxes(jnp.stack([w[8 * n : 8 * n + 8] for w in wide]), 0, 1) for n in range(3)
    ]
    rows, winds = {}, {}
    for e in range(16):
        line = window[0, e : e + 1, :] if e < 8 else beyond[0, e - 8 : e - 7, :]
        n, y = divmod(e + 4, 8)
        rows[e] = spread[n][y] * line
        if e < 4:
            rows[e] = rows[e] * below
        if e > 11:
            rows[e] = rows[e] * above
        u, v = ((low[8], low[9]), (own[8], own[9]), (beyond[1], beyond[2]))[n]
        winds[e] = tuple(0.5 * jnp.broadcast_to(w[y : y + 1], (8, 256)) for w in (u, v))
    for step in range(1, STEPS + 1):
        new = dict(rows)
        for r in range(step, 16 - step):
            hu, _ = winds[r]
            c = rows[r]
            value = (
                (1.0 - 4.0 * k) * c
                + east((k + hu) * c)
                + west((k - hu) * c)
                + (k + winds[r + 1][1]) * rows[r + 1]
                + (k - winds[r - 1][1]) * rows[r - 1]
            )
            if r < 4:
                value = value * below
            if r > 11:
                value = value * above
            new[r] = value
        rows = new
    out[...] = jnp.swapaxes(jnp.stack([rows[4 + y] for y in range(8)], axis=0), 0, 1)


def gram_block(field, binned, alpha, out):
    copies = out.shape[0]
    x = field[...].reshape(64, 256)
    count = binned[0:1, :]
    weights = jnp.concatenate([alpha[...], alpha[...]], axis=1)
    weighted = jnp.sum(weights * x, axis=0, keepdims=True) * 0.125
    forcing = binned[1:2, :] - count * weighted
    left = jnp.concatenate([x * count, jnp.broadcast_to(forcing, (8, 256))], axis=0)
    right = jnp.concatenate([x, x], axis=0)
    g = lax.dot_general(
        left, right, (((1,), (1,)), ((), ())), precision=HI, preferred_element_type=F32
    )
    lane = iota2((16, 128), 1)
    first = lane < 64
    i = iota2((16, 128), 0) + jnp.where(first, 0, 16)
    j = lane % 64
    shifted = pltpu.roll(g[32:64], 96, 1)
    top = jnp.where(first, g[0:16], g[16:32])
    low = jnp.where(first, shifted[0:16], shifted[16:32])
    packed = jnp.where((j < 32) & (i > j), low, top)
    on_diagonal = iota2((32, 128), 1) == iota2((32, 128), 0) + 96
    diagonal = jnp.sum(jnp.where(on_diagonal, g[32:64], 0.0), axis=0, keepdims=True)
    extra = jnp.where(iota2((1, 128), 1) < 64, g[64:65], diagonal)
    lines = [packed[r : r + 1] for r in range(16)] + [extra]
    halves = [jnp.concatenate(lines[h : h + 9] + [forcing], axis=1) for h in (0, 8)]
    for c in range(copies):
        out[c] = halves[2 * c // copies]


def sum_blocks(parts, first=0, stride=1):
    total = parts[first]
    for c in range(first + stride, parts.shape[0], stride):
        total = total + parts[c]
    return total


def first_sum(parts, own, core, out, window):
    half = parts.shape[0] // 2
    total = sum_blocks(parts)[:, 0:HALF]
    for c in range(out.shape[0]):
        out[c] = total
    odd = core[...] > 0.5
    for y in range(8):
        window[0, y : y + 1, :] = jnp.where(
            odd, parts[half + y][:, HALF:PACK], parts[y][:, HALF:PACK]
        )
    window[1] = own[8]
    window[2] = own[9]
    window[3] = own[12]


def next_sum(parts, out):
    total = sum_blocks(parts)
    for c in range(out.shape[0]):
        out[c] = total


def across(tile, lane):
    return jnp.broadcast_to(tile[:, lane : lane + 1], tile.shape)


def along(tile, row):
    return jnp.broadcast_to(tile[row : row + 1, :], tile.shape)


def newton_step(count, parts, alpha, factor, newton):
    upper, lower = sum_blocks(parts, 0, 2), sum_blocks(parts, 1, 2)
    total = jnp.concatenate([upper, lower[:, 128:HALF]], axis=1)
    packed = jnp.concatenate([total[:, 128 * r : 128 * r + 128] for r in range(16)], axis=0)
    extra = total[:, CORE - 128 : CORE]
    lane, sub = iota2((32, 128), 1), iota2((32, 128), 0)
    s = jnp.concatenate([packed, pltpu.roll(packed, 64, 1)], axis=0)
    top = jnp.where((lane >= sub) & (lane < 64), s, 0.0)
    diagonal = pltpu.roll(jnp.broadcast_to(extra, (32, 128)), 64, 1)
    bottom = jnp.where(
        lane == sub + 32,
        diagonal,
        jnp.where((lane >= 32) & (lane < sub + 32), pltpu.roll(s, 32, 1), 0.0),
    )
    scale = 1.0 / count
    rhs = alpha[...] - 8.0 * extra * scale
    rest = jnp.where(iota2((64, 128), 0) == 0, jnp.broadcast_to(rhs, (64, 128)), 0.0)
    z = jnp.concatenate([top, bottom, rest], axis=0)
    turned = jnp.transpose(z)[0:64]
    lanes, subs = iota2((64, 128), 1), iota2((64, 128), 0)
    both = z[0:64] + jnp.where((lanes == subs) | (lanes >= 64), 0.0, turned)
    a = jnp.where((lanes == subs) | (lanes == subs + 64), 1.0, 0.0) + both * scale
    tiles = [a[8 * t : 8 * t + 8] for t in range(8)]
    right = [across(turned[8 * t : 8 * t + 8], 64) for t in range(8)]
    lane1 = iota2((1, 128), 1)
    solved = jnp.zeros((8, 128), F32)
    for t in range(8):
        base = 8 * t
        columns = [across(tiles[t], base + c) for c in range(8)]
        e = {(i, c): along(columns[c], i) for c in range(8) for i in range(c, 8)}
        line = [along(tiles[t], q) for q in range(8)]
        b = [along(right[t], q) for q in range(8)]
        low, inverse = {}, []
        for c in range(8):
            inverse.append(1.0 / e[c, c])
            for i in range(c + 1, 8):
                low[i, c] = e[i, c] * inverse[c]
            for j in range(c + 1, 8):
                for i in range(j, 8):
                    e[i, j] = e[i, j] - low[i, c] * e[j, c]
            for i in range(c + 1, 8):
                line[i] = line[i] - low[i, c] * line[c]
                b[i] = b[i] - low[i, c] * b[c]
        for i in range(t + 1, 8):
            c_of = []
            for c in range(8):
                value = across(tiles[i], base + c)
                for j in range(c):
                    value = value - c_of[j] * low[c, j]
                c_of.append(value)
            for c in range(8):
                mult = c_of[c] * inverse[c]
                tiles[i] = tiles[i] - mult * line[c]
                right[i] = right[i] - mult * b[c]
        for q in range(8):
            solved = solved + line[q] * (b[q] * inverse[q])
            upper = line[q][0:1] * lax.rsqrt(e[q, q][0:1])
            upper = jnp.where(lane1 >= base + q, upper, 0.0)
            factor[base + q : base + q + 1, :] = upper[:, 0:64]
    newton[...] = pltpu.roll(solved, 64, 1)[0:1, 0:64]


def per_device(perturb, winds, kappa, obs_col, innov, alpha, loc_mask):
    ny = lax.axis_size("y")
    blocks = lax.axis_size(GRID)
    count = float(blocks * 8 * 256)
    sources = (
        perturb.reshape(8, 8, 256),
        winds.reshape(16, 256),
        obs_col,
        innov.reshape(8, 256),
        loc_mask,
    )
    (own,) = call(
        pack_block,
        [shape(13, 8, 256)],
        *(pltpu.with_memory_space_constraint(a, pltpu.HBM) for a in sources),
        space=pltpu.HBM,
        scratch=[pltpu.VMEM(a.shape, a.dtype) for a in sources]
        + [pltpu.SemaphoreType.DMA((len(sources),))],
    )
    low = lax.ppermute(own, GRID, [(i, (i + 1) % blocks) for i in range(blocks)])
    index = lax.axis_index(GRID)
    core = lax.axis_index("core").astype(F32).reshape(1, 1)
    joined = (index > 0).astype(F32).reshape(1, 1)
    follows = (index < blocks - 1).astype(F32).reshape(1, 1)
    mine = lax.axis_index("y").reshape(1, 1)
    k = kappa.reshape(1, 1)
    wide = jnp.concatenate([alpha, jnp.zeros((64,), F32)]).reshape(1, 128)
    evolved, binned, column = call(
        tangent,
        [shape(8, 8, 256), shape(8, 256), shape(64, 128)],
        low,
        own,
        k,
        mine,
        joined,
        wide,
        core,
        follows,
    )
    field = lax.all_to_all(evolved, "y", 0, 0, tiled=True)
    (part,) = call(gram_block, [shape(2 * ny, 1, PACK)], field, binned, column)
    parts = lax.all_to_all(part, ("core", "y"), 0, 0, tiled=True)
    part, window = call(
        first_sum,
        [shape(lax.axis_size("x"), 1, HALF), shape(4, 8, 256)],
        parts,
        own,
        core,
    )
    parts = lax.all_to_all(part, "x", 0, 0, tiled=True)
    (part,) = call(next_sum, [shape(2 * lax.axis_size("z"), 1, HALF)], parts)
    parts = lax.all_to_all(part, ("z", "core"), 0, 0, tiled=True)
    beyond = lax.ppermute(window, GRID, [((i + 1) % blocks, i) for i in range(blocks)])
    (sens,) = call(
        adjoint, [shape(8, 8, 256)], low, own, window, beyond, k, joined, follows
    )
    final = functools.partial(newton_step, count)
    final.__name__ = "newton_step"
    factor, newton = call(final, [shape(64, 64), shape(1, 64)], parts, wide)
    return factor, newton.reshape(64), sens.reshape(8, 1, 8, 256)


def solution(mesh):
    grid, mem = mesh.devices.shape
    side = int((grid // 2) ** 0.5)
    fine = Mesh(mesh.devices.reshape(side, grid // 2 // side, 2, mem), GRID + ("y",))
    in_specs = (
        P("y", None, GRID, None),
        P(None, None, GRID, None),
        P(),
        P(GRID, None),
        P(None, GRID, None),
        P(),
        P("y", GRID, None),
    )
    out_specs = (P(), P(), P("y", None, GRID, None))
    return jax.shard_map(
        per_device, mesh=fine, in_specs=in_specs, out_specs=out_specs, check_vma=False
    )
```

```python
import functools

import jax
import jax.numpy as jnp
from jax import lax
from jax.experimental import pallas as pl
from jax.experimental.pallas import tpu as pltpu
from jax.sharding import Mesh
from jax.sharding import PartitionSpec as P

STEPS = 4
F32 = jnp.float32
HI = lax.Precision.HIGHEST
GRID = ("z", "x", "core")
CORE = 17 * 128
HALF = 9 * 128
PACK = HALF + 256


def vmem():
    return pl.BlockSpec(memory_space=pltpu.VMEM)


def call(body, outs, *args, flops=1_000_000, space=pltpu.VMEM, scratch=()):
    moved = sum(a.size * 4 for a in args) + sum(o.size * 4 for o in outs)
    return pl.pallas_call(
        body,
        out_shape=outs,
        in_specs=[pl.BlockSpec(memory_space=space) for _ in args],
        out_specs=[vmem() for _ in outs],
        scratch_shapes=scratch,
        cost_estimate=pl.CostEstimate(flops=flops, bytes_accessed=moved, transcendentals=0),
        compiler_params=pltpu.CompilerParams(vmem_limit_bytes=8 * 2**20),
        name=body.__name__,
    )(*args)


def shape(*dims):
    return jax.ShapeDtypeStruct(dims, F32)


def iota2(dims, axis):
    return lax.broadcasted_iota(jnp.int32, dims, axis)


def pack_block(field, winds, col, innov, mask, out, *scratch):
    held, sems = scratch[:5], scratch[5]
    copies = [
        pltpu.make_async_copy(source, target, sems.at[n])
        for n, (source, target) in enumerate(zip((field, winds, col, innov, mask), held))
    ]
    for copy in copies:
        copy.start()
    for copy in copies:
        copy.wait()
    out[0:8] = jnp.swapaxes(held[0][...], 0, 1)
    out[8] = held[1][0:8, :]
    out[9] = held[1][8:16, :]
    out[10] = held[2][...].astype(F32)
    out[11] = held[3][...]
    out[12] = jnp.zeros((8, 256), F32)
    for m in range(8):
        out[12, :, 8 * m : 8 * m + 8] = held[4][m].astype(F32)


def east(x):
    return pltpu.roll(x, 255, 1)


def west(x):
    return pltpu.roll(x, 1, 1)


def wind_rows(blocks, r):
    u = jnp.broadcast_to(blocks[r // 8][8, r % 8 : r % 8 + 1, :], (8, 256))
    v = jnp.broadcast_to(blocks[r // 8][9, r % 8 : r % 8 + 1, :], (8, 256))
    return 0.5 * u, 0.5 * v


def select_row(tile, sub, mine):
    return jnp.sum(jnp.where(sub == mine, tile, 0.0), axis=0, keepdims=True)


def tangent(low, own, kappa, mine, joined, alpha, core, follows, out, binned, column_of):
    column_of[...] = jnp.transpose(jnp.broadcast_to(alpha[...], (128, 128)))[0:64]
    blocks = (low, own)
    k = jnp.broadcast_to(kappa[...], (8, 256))
    joint = jnp.broadcast_to(joined[...], (8, 256))
    rows = [blocks[r // 8][r % 8] for r in range(16)]
    winds = [wind_rows(blocks, r) for r in range(16)]
    for step in range(1, STEPS + 1):
        new = list(rows)
        for r in range(step, 16 - step):
            hu, hv = winds[r]
            c = rows[r]
            north = (k - hv) * rows[r + 1]
            south = (k + hv) * rows[r - 1]
            if r == 7:
                north = north * joint
            if r == 8:
                south = south * joint
            new[r] = (
                (1.0 - 4.0 * k) * c + (k - hu) * east(c) + (k + hu) * west(c) + north + south
            )
        rows = new
    for y in range(8):
        out[y] = rows[4 + y]
    sub = iota2((8, 256), 0)
    turned = [
        jnp.where(sub < 4, pltpu.roll(low[tile], 4, 0), pltpu.roll(own[tile], 4, 0))
        for tile in (10, 11)
    ]
    column, value = (select_row(tile, sub, mine[...]) for tile in turned)
    hit = (iota2((256, 256), 0).astype(F32) == column).astype(F32)
    values = jnp.where(sub == 0, 1.0, jnp.broadcast_to(value, (8, 256)))
    binned[...] = lax.dot_general(
        values, hit, (((1,), (1,)), ((), ())), precision=HI, preferred_element_type=F32
    )


def adjoint(low, own, window, beyond, kappa, joined, follows, out):
    k = jnp.broadcast_to(kappa[...], (8, 256))
    below = jnp.broadcast_to(joined[...], (8, 256))
    above = jnp.broadcast_to(follows[...], (8, 256))
    masks = jnp.concatenate([b[:, 0:128] for b in (low[12], own[12], beyond[3])], axis=0)
    wide = []
    for m in range(8):
        expand = (iota2((128, 256), 0) == 8 * m + iota2((128, 256), 1) // 32).astype(F32)
        wide.append(jnp.dot(masks, expand, preferred_element_type=F32))
    spread = [
        jnp.swapaxes(jnp.stack([w[8 * n : 8 * n + 8] for w in wide]), 0, 1) for n in range(3)
    ]
    rows, winds = {}, {}
    for e in range(16):
        line = window[0, e : e + 1, :] if e < 8 else beyond[0, e - 8 : e - 7, :]
        n, y = divmod(e + 4, 8)
        rows[e] = spread[n][y] * line
        if e < 4:
            rows[e] = rows[e] * below
        if e > 11:
            rows[e] = rows[e] * above
        u, v = ((low[8], low[9]), (own[8], own[9]), (beyond[1], beyond[2]))[n]
        winds[e] = tuple(0.5 * jnp.broadcast_to(w[y : y + 1], (8, 256)) for w in (u, v))
    for step in range(1, STEPS + 1):
        new = dict(rows)
        for r in range(step, 16 - step):
            hu, _ = winds[r]
            c = rows[r]
            value = (
                (1.0 - 4.0 * k) * c
                + east((k + hu) * c)
                + west((k - hu) * c)
                + (k + winds[r + 1][1]) * rows[r + 1]
                + (k - winds[r - 1][1]) * rows[r - 1]
            )
            if r < 4:
                value = value * below
            if r > 11:
                value = value * above
            new[r] = value
        rows = new
    out[...] = jnp.swapaxes(jnp.stack([rows[4 + y] for y in range(8)], axis=0), 0, 1)


def gram_block(field, binned, alpha, out):
    copies = out.shape[0]
    x = field[...].reshape(64, 256)
    count = binned[0:1, :]
    weights = jnp.concatenate([alpha[...], alpha[...]], axis=1)
    weighted = jnp.sum(weights * x, axis=0, keepdims=True) * 0.125
    forcing = binned[1:2, :] - count * weighted
    left = jnp.concatenate([x * count, jnp.broadcast_to(forcing, (8, 256))], axis=0)
    right = jnp.concatenate([x, x], axis=0)
    g = lax.dot_general(
        left, right, (((1,), (1,)), ((), ())), precision=HI, preferred_element_type=F32
    )
    lane = iota2((16, 128), 1)
    first = lane < 64
    i = iota2((16, 128), 0) + jnp.where(first, 0, 16)
    j = lane % 64
    shifted = pltpu.roll(g[32:64], 96, 1)
    top = jnp.where(first, g[0:16], g[16:32])
    low = jnp.where(first, shifted[0:16], shifted[16:32])
    packed = jnp.where((j < 32) & (i > j), low, top)
    on_diagonal = iota2((32, 128), 1) == iota2((32, 128), 0) + 96
    diagonal = jnp.sum(jnp.where(on_diagonal, g[32:64], 0.0), axis=0, keepdims=True)
    extra = jnp.where(iota2((1, 128), 1) < 64, g[64:65], diagonal)
    lines = [packed[r : r + 1] for r in range(16)] + [extra]
    halves = [jnp.concatenate(lines[h : h + 9] + [forcing], axis=1) for h in (0, 8)]
    for c in range(copies):
        out[c] = halves[2 * c // copies]


def sum_blocks(parts, first=0, stride=1):
    total = parts[first]
    for c in range(first + stride, parts.shape[0], stride):
        total = total + parts[c]
    return total


def first_sum(parts, own, core, out, window):
    half = parts.shape[0] // 2
    total = sum_blocks(parts)[:, 0:HALF]
    for c in range(out.shape[0]):
        out[c] = total
    odd = core[...] > 0.5
    for y in range(8):
        window[0, y : y + 1, :] = jnp.where(
            odd, parts[half + y][:, HALF:PACK], parts[y][:, HALF:PACK]
        )
    window[1] = own[8]
    window[2] = own[9]
    window[3] = own[12]


def next_sum(parts, out):
    total = sum_blocks(parts)
    for c in range(out.shape[0]):
        out[c] = total


def across(tile, lane):
    return jnp.broadcast_to(tile[:, lane : lane + 1], tile.shape)


def along(tile, row):
    return jnp.broadcast_to(tile[row : row + 1, :], tile.shape)


def newton_step(count, parts, alpha, factor, newton):
    upper, lower = sum_blocks(parts, 0, 2), sum_blocks(parts, 1, 2)
    total = jnp.concatenate([upper, lower[:, 128:HALF]], axis=1)
    packed = jnp.concatenate([total[:, 128 * r : 128 * r + 128] for r in range(16)], axis=0)
    extra = total[:, CORE - 128 : CORE]
    lane, sub = iota2((32, 128), 1), iota2((32, 128), 0)
    s = jnp.concatenate([packed, pltpu.roll(packed, 64, 1)], axis=0)
    top = jnp.where((lane >= sub) & (lane < 64), s, 0.0)
    diagonal = pltpu.roll(jnp.broadcast_to(extra, (32, 128)), 64, 1)
    bottom = jnp.where(
        lane == sub + 32,
        diagonal,
        jnp.where((lane >= 32) & (lane < sub + 32), pltpu.roll(s, 32, 1), 0.0),
    )
    scale = 1.0 / count
    rhs = alpha[...] - 8.0 * extra * scale
    rest = jnp.where(iota2((64, 128), 0) == 0, jnp.broadcast_to(rhs, (64, 128)), 0.0)
    z = jnp.concatenate([top, bottom, rest], axis=0)
    turned = jnp.transpose(z)[0:64]
    lanes, subs = iota2((64, 128), 1), iota2((64, 128), 0)
    both = z[0:64] + jnp.where((lanes == subs) | (lanes >= 64), 0.0, turned)
    a = jnp.where((lanes == subs) | (lanes == subs + 64), 1.0, 0.0) + both * scale
    tiles = [a[8 * t : 8 * t + 8] for t in range(8)]
    right = [across(turned[8 * t : 8 * t + 8], 64) for t in range(8)]
    lane1 = iota2((1, 128), 1)
    solved = jnp.zeros((8, 128), F32)
    for t in range(8):
        base = 8 * t
        columns = [across(tiles[t], base + c) for c in range(8)]
        e = {(i, c): along(columns[c], i) for c in range(8) for i in range(c, 8)}
        line = [along(tiles[t], q) for q in range(8)]
        b = [along(right[t], q) for q in range(8)]
        low, inverse = {}, []
        for c in range(8):
            inverse.append(1.0 / e[c, c])
            for i in range(c + 1, 8):
                low[i, c] = e[i, c] * inverse[c]
            for j in range(c + 1, 8):
                for i in range(j, 8):
                    e[i, j] = e[i, j] - low[i, c] * e[j, c]
            for i in range(c + 1, 8):
                line[i] = line[i] - low[i, c] * line[c]
                b[i] = b[i] - low[i, c] * b[c]
        for i in range(t + 1, 8):
            c_of = []
            for c in range(8):
                value = across(tiles[i], base + c)
                for j in range(c):
                    value = value - c_of[j] * low[c, j]
                c_of.append(value)
            for c in range(8):
                mult = c_of[c] * inverse[c]
                tiles[i] = tiles[i] - mult * line[c]
                right[i] = right[i] - mult * b[c]
        for q in range(8):
            solved = solved + line[q] * (b[q] * inverse[q])
            upper = line[q][0:1] * lax.rsqrt(e[q, q][0:1])
            upper = jnp.where(lane1 >= base + q, upper, 0.0)
            factor[base + q : base + q + 1, :] = upper[:, 0:64]
    newton[...] = pltpu.roll(solved, 64, 1)[0:1, 0:64]


def finish(
    count, parts, alpha, low, own, window, beyond, kappa, joined, follows, factor, newton, sens
):
    adjoint(low, own, window, beyond, kappa, joined, follows, sens)
    newton_step(count, parts, alpha, factor, newton)


def per_device(perturb, winds, kappa, obs_col, innov, alpha, loc_mask):
    ny = lax.axis_size("y")
    blocks = lax.axis_size(GRID)
    count = float(blocks * 8 * 256)
    sources = (
        perturb.reshape(8, 8, 256),
        winds.reshape(16, 256),
        obs_col,
        innov.reshape(8, 256),
        loc_mask,
    )
    (own,) = call(
        pack_block,
        [shape(13, 8, 256)],
        *(pltpu.with_memory_space_constraint(a, pltpu.HBM) for a in sources),
        space=pltpu.HBM,
        scratch=[pltpu.VMEM(a.shape, a.dtype) for a in sources]
        + [pltpu.SemaphoreType.DMA((len(sources),))],
    )
    low = lax.ppermute(own, GRID, [(i, (i + 1) % blocks) for i in range(blocks)])
    index = lax.axis_index(GRID)
    core = lax.axis_index("core").astype(F32).reshape(1, 1)
    joined = (index > 0).astype(F32).reshape(1, 1)
    follows = (index < blocks - 1).astype(F32).reshape(1, 1)
    mine = lax.axis_index("y").reshape(1, 1)
    k = kappa.reshape(1, 1)
    wide = jnp.concatenate([alpha, jnp.zeros((64,), F32)]).reshape(1, 128)
    evolved, binned, column = call(
        tangent,
        [shape(8, 8, 256), shape(8, 256), shape(64, 128)],
        low,
        own,
        k,
        mine,
        joined,
        wide,
        core,
        follows,
    )
    field = lax.all_to_all(evolved, "y", 0, 0, tiled=True)
    (part,) = call(gram_block, [shape(2 * ny, 1, PACK)], field, binned, column)
    parts = lax.all_to_all(part, ("core", "y"), 0, 0, tiled=True)
    part, window = call(
        first_sum,
        [shape(lax.axis_size("x"), 1, HALF), shape(4, 8, 256)],
        parts,
        own,
        core,
    )
    parts = lax.all_to_all(part, "x", 0, 0, tiled=True)
    (part,) = call(next_sum, [shape(2 * lax.axis_size("z"), 1, HALF)], parts)
    parts = lax.all_to_all(part, ("z", "core"), 0, 0, tiled=True)
    beyond = lax.ppermute(window, GRID, [((i + 1) % blocks, i) for i in range(blocks)])
    last = functools.partial(finish, count)
    last.__name__ = "finish"
    factor, newton, sens = call(
        last,
        [shape(64, 64), shape(1, 64), shape(8, 8, 256)],
        parts,
        wide,
        low,
        own,
        window,
        beyond,
        k,
        joined,
        follows,
    )
    return factor, newton.reshape(64), sens.reshape(8, 1, 8, 256)


def solution(mesh):
    grid, mem = mesh.devices.shape
    side = int((grid // 2) ** 0.5)
    fine = Mesh(mesh.devices.reshape(side, grid // 2 // side, 2, mem), GRID + ("y",))
    in_specs = (
        P("y", None, GRID, None),
        P(None, None, GRID, None),
        P(),
        P(GRID, None),
        P(None, GRID, None),
        P(),
        P("y", GRID, None),
    )
    out_specs = (P(), P(), P("y", None, GRID, None))
    return jax.shard_map(
        per_device, mesh=fine, in_specs=in_specs, out_specs=out_specs, check_vma=False
    )
```

```python
import functools

import jax
import jax.numpy as jnp
from jax import lax
from jax.experimental import pallas as pl
from jax.experimental.pallas import tpu as pltpu
from jax.sharding import Mesh
from jax.sharding import PartitionSpec as P

STEPS = 4
F32 = jnp.float32
HI = lax.Precision.HIGHEST
GRID = ("z", "x", "core")
CORE = 17 * 128
HALF = 9 * 128
PACK = HALF + 256


def vmem():
    return pl.BlockSpec(memory_space=pltpu.VMEM)


def call(body, outs, *args, flops=1_000_000, space=pltpu.VMEM, scratch=()):
    moved = sum(a.size * 4 for a in args) + sum(o.size * 4 for o in outs)
    return pl.pallas_call(
        body,
        out_shape=outs,
        in_specs=[pl.BlockSpec(memory_space=space) for _ in args],
        out_specs=[vmem() for _ in outs],
        scratch_shapes=scratch,
        cost_estimate=pl.CostEstimate(flops=flops, bytes_accessed=moved, transcendentals=0),
        compiler_params=pltpu.CompilerParams(vmem_limit_bytes=8 * 2**20),
        name=body.__name__,
    )(*args)


def shape(*dims):
    return jax.ShapeDtypeStruct(dims, F32)


def iota2(dims, axis):
    return lax.broadcasted_iota(jnp.int32, dims, axis)


def pack_block(field, winds, col, innov, mask, out, near, *scratch):
    held, sems = scratch[:5], scratch[5]
    copies = [
        pltpu.make_async_copy(source, target, sems.at[n])
        for n, (source, target) in enumerate(zip((field, winds, col, innov, mask), held))
    ]
    for copy in copies:
        copy.start()
    for n in (2, 3, 1, 4):
        copies[n].wait()
    near[0, 4:8, :] = held[2][0:4, :].astype(F32)
    near[1, 4:8, :] = held[3][0:4, :]
    near[:, 0:4, :] = jnp.zeros((2, 4, 256), F32)
    out[8] = held[1][0:8, :]
    out[9] = held[1][8:16, :]
    out[10, 0:4, :] = held[2][4:8, :].astype(F32)
    out[10, 4:8, :] = held[3][4:8, :]
    out[11] = jnp.zeros((8, 256), F32)
    for m in range(8):
        out[11, :, 8 * m : 8 * m + 8] = held[4][m].astype(F32)
    copies[0].wait()
    out[0:8] = jnp.swapaxes(held[0][...], 0, 1)


def east(x):
    return pltpu.roll(x, 255, 1)


def west(x):
    return pltpu.roll(x, 1, 1)


def wind_rows(blocks, r):
    u = jnp.broadcast_to(blocks[r // 8][8, r % 8 : r % 8 + 1, :], (8, 256))
    v = jnp.broadcast_to(blocks[r // 8][9, r % 8 : r % 8 + 1, :], (8, 256))
    return 0.5 * u, 0.5 * v


def select_row(tile, sub, mine):
    return jnp.sum(jnp.where(sub == mine, tile, 0.0), axis=0, keepdims=True)


def tangent(low, own, near, kappa, mine, joined, alpha, core, follows, out, binned, column_of):
    column_of[...] = jnp.transpose(jnp.broadcast_to(alpha[...], (128, 128)))[0:64]
    blocks = (low, own)
    k = jnp.broadcast_to(kappa[...], (8, 256))
    joint = jnp.broadcast_to(joined[...], (8, 256))
    rows = [blocks[r // 8][r % 8] for r in range(16)]
    winds = [wind_rows(blocks, r) for r in range(16)]
    for step in range(1, STEPS + 1):
        new = list(rows)
        for r in range(step, 16 - step):
            hu, hv = winds[r]
            c = rows[r]
            north = (k - hv) * rows[r + 1]
            south = (k + hv) * rows[r - 1]
            if r == 7:
                north = north * joint
            if r == 8:
                south = south * joint
            new[r] = (
                (1.0 - 4.0 * k) * c + (k - hu) * east(c) + (k + hu) * west(c) + north + south
            )
        rows = new
    for y in range(8):
        out[y] = rows[4 + y]
    sub = iota2((8, 256), 0)
    turned = (
        jnp.where(sub < 4, low[10], near[0]),
        jnp.where(sub < 4, pltpu.roll(low[10], 4, 0), near[1]),
    )
    column, value = (select_row(tile, sub, mine[...]) for tile in turned)
    hit = (iota2((256, 256), 0).astype(F32) == column).astype(F32)
    values = jnp.where(sub == 0, 1.0, jnp.broadcast_to(value, (8, 256)))
    binned[...] = lax.dot_general(
        values, hit, (((1,), (1,)), ((), ())), precision=HI, preferred_element_type=F32
    )


def adjoint(low, own, window, beyond, kappa, joined, follows, out):
    k = jnp.broadcast_to(kappa[...], (8, 256))
    below = jnp.broadcast_to(joined[...], (8, 256))
    above = jnp.broadcast_to(follows[...], (8, 256))
    masks = jnp.concatenate([b[:, 0:128] for b in (low[11], own[11], beyond[3])], axis=0)
    wide = []
    for m in range(8):
        expand = (iota2((128, 256), 0) == 8 * m + iota2((128, 256), 1) // 32).astype(F32)
        wide.append(jnp.dot(masks, expand, preferred_element_type=F32))
    spread = [
        jnp.swapaxes(jnp.stack([w[8 * n : 8 * n + 8] for w in wide]), 0, 1) for n in range(3)
    ]
    rows, winds = {}, {}
    for e in range(16):
        line = window[0, e : e + 1, :] if e < 8 else beyond[0, e - 8 : e - 7, :]
        n, y = divmod(e + 4, 8)
        rows[e] = spread[n][y] * line
        if e < 4:
            rows[e] = rows[e] * below
        if e > 11:
            rows[e] = rows[e] * above
        u, v = ((low[8], low[9]), (own[8], own[9]), (beyond[1], beyond[2]))[n]
        winds[e] = tuple(0.5 * jnp.broadcast_to(w[y : y + 1], (8, 256)) for w in (u, v))
    for step in range(1, STEPS + 1):
        new = dict(rows)
        for r in range(step, 16 - step):
            hu, _ = winds[r]
            c = rows[r]
            value = (
                (1.0 - 4.0 * k) * c
                + east((k + hu) * c)
                + west((k - hu) * c)
                + (k + winds[r + 1][1]) * rows[r + 1]
                + (k - winds[r - 1][1]) * rows[r - 1]
            )
            if r < 4:
                value = value * below
            if r > 11:
                value = value * above
            new[r] = value
        rows = new
    out[...] = jnp.swapaxes(jnp.stack([rows[4 + y] for y in range(8)], axis=0), 0, 1)


def gram_block(field, binned, alpha, out):
    copies = out.shape[0]
    x = field[...].reshape(64, 256)
    count = binned[0:1, :]
    weights = jnp.concatenate([alpha[...], alpha[...]], axis=1)
    weighted = jnp.sum(weights * x, axis=0, keepdims=True) * 0.125
    forcing = binned[1:2, :] - count * weighted
    left = jnp.concatenate([x * count, jnp.broadcast_to(forcing, (8, 256))], axis=0)
    right = jnp.concatenate([x, x], axis=0)
    g = lax.dot_general(
        left, right, (((1,), (1,)), ((), ())), precision=HI, preferred_element_type=F32
    )
    lane = iota2((16, 128), 1)
    first = lane < 64
    i = iota2((16, 128), 0) + jnp.where(first, 0, 16)
    j = lane % 64
    shifted = pltpu.roll(g[32:64], 96, 1)
    top = jnp.where(first, g[0:16], g[16:32])
    low = jnp.where(first, shifted[0:16], shifted[16:32])
    packed = jnp.where((j < 32) & (i > j), low, top)
    on_diagonal = iota2((32, 128), 1) == iota2((32, 128), 0) + 96
    diagonal = jnp.sum(jnp.where(on_diagonal, g[32:64], 0.0), axis=0, keepdims=True)
    extra = jnp.where(iota2((1, 128), 1) < 64, g[64:65], diagonal)
    lines = [packed[r : r + 1] for r in range(16)] + [extra]
    halves = [jnp.concatenate(lines[h : h + 9] + [forcing], axis=1) for h in (0, 8)]
    for c in range(copies):
        out[c] = halves[2 * c // copies]


def sum_blocks(parts, first=0, stride=1):
    total = parts[first]
    for c in range(first + stride, parts.shape[0], stride):
        total = total + parts[c]
    return total


def first_sum(parts, own, core, out, window):
    half = parts.shape[0] // 2
    total = sum_blocks(parts)[:, 0:HALF]
    for c in range(out.shape[0]):
        out[c] = total
    odd = core[...] > 0.5
    for y in range(8):
        window[0, y : y + 1, :] = jnp.where(
            odd, parts[half + y][:, HALF:PACK], parts[y][:, HALF:PACK]
        )
    window[1] = own[8]
    window[2] = own[9]
    window[3] = own[11]


def next_sum(parts, out):
    total = sum_blocks(parts)
    for c in range(out.shape[0]):
        out[c] = total


def across(tile, lane):
    return jnp.broadcast_to(tile[:, lane : lane + 1], tile.shape)


def along(tile, row):
    return jnp.broadcast_to(tile[row : row + 1, :], tile.shape)


def newton_step(count, parts, alpha, factor, newton):
    upper, lower = sum_blocks(parts, 0, 2), sum_blocks(parts, 1, 2)
    total = jnp.concatenate([upper, lower[:, 128:HALF]], axis=1)
    packed = jnp.concatenate([total[:, 128 * r : 128 * r + 128] for r in range(16)], axis=0)
    extra = total[:, CORE - 128 : CORE]
    lane, sub = iota2((32, 128), 1), iota2((32, 128), 0)
    s = jnp.concatenate([packed, pltpu.roll(packed, 64, 1)], axis=0)
    top = jnp.where((lane >= sub) & (lane < 64), s, 0.0)
    diagonal = pltpu.roll(jnp.broadcast_to(extra, (32, 128)), 64, 1)
    bottom = jnp.where(
        lane == sub + 32,
        diagonal,
        jnp.where((lane >= 32) & (lane < sub + 32), pltpu.roll(s, 32, 1), 0.0),
    )
    scale = 1.0 / count
    rhs = alpha[...] - 8.0 * extra * scale
    rest = jnp.where(iota2((64, 128), 0) == 0, jnp.broadcast_to(rhs, (64, 128)), 0.0)
    z = jnp.concatenate([top, bottom, rest], axis=0)
    turned = jnp.transpose(z)[0:64]
    lanes, subs = iota2((64, 128), 1), iota2((64, 128), 0)
    both = z[0:64] + jnp.where((lanes == subs) | (lanes >= 64), 0.0, turned)
    a = jnp.where((lanes == subs) | (lanes == subs + 64), 1.0, 0.0) + both * scale
    tiles = [a[8 * t : 8 * t + 8] for t in range(8)]
    right = [across(turned[8 * t : 8 * t + 8], 64) for t in range(8)]
    lane1 = iota2((1, 128), 1)
    solved = jnp.zeros((8, 128), F32)
    for t in range(8):
        base = 8 * t
        columns = [across(tiles[t], base + c) for c in range(8)]
        e = {(i, c): along(columns[c], i) for c in range(8) for i in range(c, 8)}
        line = [along(tiles[t], q) for q in range(8)]
        b = [along(right[t], q) for q in range(8)]
        low, inverse = {}, []
        for c in range(8):
            inverse.append(1.0 / e[c, c])
            for i in range(c + 1, 8):
                low[i, c] = e[i, c] * inverse[c]
            for j in range(c + 1, 8):
                for i in range(j, 8):
                    e[i, j] = e[i, j] - low[i, c] * e[j, c]
            for i in range(c + 1, 8):
                line[i] = line[i] - low[i, c] * line[c]
                b[i] = b[i] - low[i, c] * b[c]
        for i in range(t + 1, 8):
            c_of = []
            for c in range(8):
                value = across(tiles[i], base + c)
                for j in range(c):
                    value = value - c_of[j] * low[c, j]
                c_of.append(value)
            for c in range(8):
                mult = c_of[c] * inverse[c]
                tiles[i] = tiles[i] - mult * line[c]
                right[i] = right[i] - mult * b[c]
        for q in range(8):
            solved = solved + line[q] * (b[q] * inverse[q])
            upper = line[q][0:1] * lax.rsqrt(e[q, q][0:1])
            upper = jnp.where(lane1 >= base + q, upper, 0.0)
            factor[base + q : base + q + 1, :] = upper[:, 0:64]
    newton[...] = pltpu.roll(solved, 64, 1)[0:1, 0:64]


def per_device(perturb, winds, kappa, obs_col, innov, alpha, loc_mask):
    ny = lax.axis_size("y")
    blocks = lax.axis_size(GRID)
    count = float(blocks * 8 * 256)
    sources = (
        perturb.reshape(8, 8, 256),
        winds.reshape(16, 256),
        obs_col,
        innov.reshape(8, 256),
        loc_mask,
    )
    own, near = call(
        pack_block,
        [shape(12, 8, 256), shape(2, 8, 256)],
        *(pltpu.with_memory_space_constraint(a, pltpu.HBM) for a in sources),
        space=pltpu.HBM,
        scratch=[pltpu.VMEM(a.shape, a.dtype) for a in sources]
        + [pltpu.SemaphoreType.DMA((len(sources),))],
    )
    low = lax.ppermute(own, GRID, [(i, (i + 1) % blocks) for i in range(blocks)])
    index = lax.axis_index(GRID)
    core = lax.axis_index("core").astype(F32).reshape(1, 1)
    joined = (index > 0).astype(F32).reshape(1, 1)
    follows = (index < blocks - 1).astype(F32).reshape(1, 1)
    mine = lax.axis_index("y").reshape(1, 1)
    k = kappa.reshape(1, 1)
    wide = jnp.concatenate([alpha, jnp.zeros((64,), F32)]).reshape(1, 128)
    evolved, binned, column = call(
        tangent,
        [shape(8, 8, 256), shape(8, 256), shape(64, 128)],
        low,
        own,
        near,
        k,
        mine,
        joined,
        wide,
        core,
        follows,
    )
    field = lax.all_to_all(evolved, "y", 0, 0, tiled=True)
    (part,) = call(gram_block, [shape(2 * ny, 1, PACK)], field, binned, column)
    parts = lax.all_to_all(part, ("core", "y"), 0, 0, tiled=True)
    part, window = call(
        first_sum,
        [shape(lax.axis_size("x"), 1, HALF), shape(4, 8, 256)],
        parts,
        own,
        core,
    )
    parts = lax.all_to_all(part, "x", 0, 0, tiled=True)
    (part,) = call(next_sum, [shape(2 * lax.axis_size("z"), 1, HALF)], parts)
    parts = lax.all_to_all(part, ("z", "core"), 0, 0, tiled=True)
    beyond = lax.ppermute(window, GRID, [((i + 1) % blocks, i) for i in range(blocks)])
    (sens,) = call(
        adjoint, [shape(8, 8, 256)], low, own, window, beyond, k, joined, follows
    )
    final = functools.partial(newton_step, count)
    final.__name__ = "newton_step"
    factor, newton = call(final, [shape(64, 64), shape(1, 64)], parts, wide)
    return factor, newton.reshape(64), sens.reshape(8, 1, 8, 256)


def solution(mesh):
    grid, mem = mesh.devices.shape
    side = int((grid // 2) ** 0.5)
    fine = Mesh(mesh.devices.reshape(side, grid // 2 // side, 2, mem), GRID + ("y",))
    in_specs = (
        P("y", None, GRID, None),
        P(None, None, GRID, None),
        P(),
        P(GRID, None),
        P(None, GRID, None),
        P(),
        P("y", GRID, None),
    )
    out_specs = (P(), P(), P("y", None, GRID, None))
    return jax.shard_map(
        per_device, mesh=fine, in_specs=in_specs, out_specs=out_specs, check_vma=False
    )
```

```python
import functools

import jax
import jax.numpy as jnp
from jax import lax
from jax.experimental import pallas as pl
from jax.experimental.pallas import tpu as pltpu
from jax.sharding import Mesh
from jax.sharding import PartitionSpec as P

STEPS = 4
F32 = jnp.float32
HI = lax.Precision.HIGHEST
GRID = ("z", "x", "core")
CORE = 17 * 128
HALF = 9 * 128
PACK = CORE + 256


def vmem():
    return pl.BlockSpec(memory_space=pltpu.VMEM)


def call(body, outs, *args, flops=1_000_000, space=pltpu.VMEM, scratch=()):
    moved = sum(a.size * 4 for a in args) + sum(o.size * 4 for o in outs)
    return pl.pallas_call(
        body,
        out_shape=outs,
        in_specs=[pl.BlockSpec(memory_space=space) for _ in args],
        out_specs=[vmem() for _ in outs],
        scratch_shapes=scratch,
        cost_estimate=pl.CostEstimate(flops=flops, bytes_accessed=moved, transcendentals=0),
        compiler_params=pltpu.CompilerParams(vmem_limit_bytes=8 * 2**20),
        name=body.__name__,
    )(*args)


def shape(*dims):
    return jax.ShapeDtypeStruct(dims, F32)


def iota2(dims, axis):
    return lax.broadcasted_iota(jnp.int32, dims, axis)


def pack_block(field, winds, col, innov, mask, out, near, *scratch):
    held, sems = scratch[:5], scratch[5]
    copies = [
        pltpu.make_async_copy(source, target, sems.at[n])
        for n, (source, target) in enumerate(zip((field, winds, col, innov, mask), held))
    ]
    for copy in copies:
        copy.start()
    for n in (2, 3, 1, 4):
        copies[n].wait()
    near[0, 4:8, :] = held[2][0:4, :].astype(F32)
    near[1, 4:8, :] = held[3][0:4, :]
    near[:, 0:4, :] = jnp.zeros((2, 4, 256), F32)
    out[8] = held[1][0:8, :]
    out[9] = held[1][8:16, :]
    out[10, 0:4, :] = held[2][4:8, :].astype(F32)
    out[10, 4:8, :] = held[3][4:8, :]
    out[11] = jnp.zeros((8, 256), F32)
    for m in range(8):
        out[11, :, 8 * m : 8 * m + 8] = held[4][m].astype(F32)
    copies[0].wait()
    out[0:8] = jnp.swapaxes(held[0][...], 0, 1)


def east(x):
    return pltpu.roll(x, 255, 1)


def west(x):
    return pltpu.roll(x, 1, 1)


def wind_rows(blocks, r):
    u = jnp.broadcast_to(blocks[r // 8][8, r % 8 : r % 8 + 1, :], (8, 256))
    v = jnp.broadcast_to(blocks[r // 8][9, r % 8 : r % 8 + 1, :], (8, 256))
    return 0.5 * u, 0.5 * v


def select_row(tile, sub, mine):
    return jnp.sum(jnp.where(sub == mine, tile, 0.0), axis=0, keepdims=True)


def tangent(low, own, near, kappa, mine, joined, alpha, follows, out, binned, column_of):
    column_of[...] = jnp.transpose(jnp.broadcast_to(alpha[...], (128, 128)))[0:64]
    blocks = (low, own)
    k = jnp.broadcast_to(kappa[...], (8, 256))
    joint = jnp.broadcast_to(joined[...], (8, 256))
    rows = [blocks[r // 8][r % 8] for r in range(16)]
    winds = [wind_rows(blocks, r) for r in range(16)]
    for step in range(1, STEPS + 1):
        new = list(rows)
        for r in range(step, 16 - step):
            hu, hv = winds[r]
            c = rows[r]
            north = (k - hv) * rows[r + 1]
            south = (k + hv) * rows[r - 1]
            if r == 7:
                north = north * joint
            if r == 8:
                south = south * joint
            new[r] = (
                (1.0 - 4.0 * k) * c + (k - hu) * east(c) + (k + hu) * west(c) + north + south
            )
        rows = new
    for y in range(8):
        out[y] = rows[4 + y]
    sub = iota2((8, 256), 0)
    turned = (
        jnp.where(sub < 4, low[10], near[0]),
        jnp.where(sub < 4, pltpu.roll(low[10], 4, 0), near[1]),
    )
    column, value = (select_row(tile, sub, mine[...]) for tile in turned)
    hit = (iota2((256, 256), 0).astype(F32) == column).astype(F32)
    values = jnp.where(sub == 0, 1.0, jnp.broadcast_to(value, (8, 256)))
    binned[...] = lax.dot_general(
        values, hit, (((1,), (1,)), ((), ())), precision=HI, preferred_element_type=F32
    )


def adjoint(low, own, window, beyond, kappa, joined, follows, out):
    k = jnp.broadcast_to(kappa[...], (8, 256))
    below = jnp.broadcast_to(joined[...], (8, 256))
    above = jnp.broadcast_to(follows[...], (8, 256))
    masks = jnp.concatenate([b[:, 0:128] for b in (low[11], own[11], beyond[3])], axis=0)
    wide = []
    for m in range(8):
        expand = (iota2((128, 256), 0) == 8 * m + iota2((128, 256), 1) // 32).astype(F32)
        wide.append(jnp.dot(masks, expand, preferred_element_type=F32))
    spread = [
        jnp.swapaxes(jnp.stack([w[8 * n : 8 * n + 8] for w in wide]), 0, 1) for n in range(3)
    ]
    rows, winds = {}, {}
    for e in range(16):
        line = window[0, e : e + 1, :] if e < 8 else beyond[0, e - 8 : e - 7, :]
        n, y = divmod(e + 4, 8)
        rows[e] = spread[n][y] * line
        if e < 4:
            rows[e] = rows[e] * below
        if e > 11:
            rows[e] = rows[e] * above
        u, v = ((low[8], low[9]), (own[8], own[9]), (beyond[1], beyond[2]))[n]
        winds[e] = tuple(0.5 * jnp.broadcast_to(w[y : y + 1], (8, 256)) for w in (u, v))
    for step in range(1, STEPS + 1):
        new = dict(rows)
        for r in range(step, 16 - step):
            hu, _ = winds[r]
            c = rows[r]
            value = (
                (1.0 - 4.0 * k) * c
                + east((k + hu) * c)
                + west((k - hu) * c)
                + (k + winds[r + 1][1]) * rows[r + 1]
                + (k - winds[r - 1][1]) * rows[r - 1]
            )
            if r < 4:
                value = value * below
            if r > 11:
                value = value * above
            new[r] = value
        rows = new
    out[...] = jnp.swapaxes(jnp.stack([rows[4 + y] for y in range(8)], axis=0), 0, 1)


def gram_block(field, binned, alpha, out):
    copies = out.shape[0]
    x = field[...].reshape(64, 256)
    count = binned[0:1, :]
    weights = jnp.concatenate([alpha[...], alpha[...]], axis=1)
    weighted = jnp.sum(weights * x, axis=0, keepdims=True) * 0.125
    forcing = binned[1:2, :] - count * weighted
    left = jnp.concatenate([x * count, jnp.broadcast_to(forcing, (8, 256))], axis=0)
    right = jnp.concatenate([x, x], axis=0)
    g = lax.dot_general(
        left, right, (((1,), (1,)), ((), ())), precision=HI, preferred_element_type=F32
    )
    lane = iota2((16, 128), 1)
    first = lane < 64
    i = iota2((16, 128), 0) + jnp.where(first, 0, 16)
    j = lane % 64
    shifted = pltpu.roll(g[32:64], 96, 1)
    top = jnp.where(first, g[0:16], g[16:32])
    low = jnp.where(first, shifted[0:16], shifted[16:32])
    packed = jnp.where((j < 32) & (i > j), low, top)
    on_diagonal = iota2((32, 128), 1) == iota2((32, 128), 0) + 96
    diagonal = jnp.sum(jnp.where(on_diagonal, g[32:64], 0.0), axis=0, keepdims=True)
    extra = jnp.where(iota2((1, 128), 1) < 64, g[64:65], diagonal)
    lines = [packed[r : r + 1] for r in range(16)] + [extra]
    flat = jnp.concatenate(lines + [forcing], axis=1)
    for c in range(copies):
        out[c] = flat


def sum_blocks(parts, first=0, stride=1):
    total = parts[first]
    for c in range(first + stride, parts.shape[0], stride):
        total = total + parts[c]
    return total


def first_sum(parts, own, out, window):
    total = sum_blocks(parts)
    halves = (total[:, 0:HALF], total[:, CORE - HALF : CORE])
    for c in range(out.shape[0]):
        out[c] = halves[c % 2]
    for y in range(8):
        window[0, y : y + 1, :] = parts[y][:, CORE:PACK]
    window[1] = own[8]
    window[2] = own[9]
    window[3] = own[11]


def next_sum(parts, out):
    total = sum_blocks(parts)
    for c in range(out.shape[0]):
        out[c] = total


def across(tile, lane):
    return jnp.broadcast_to(tile[:, lane : lane + 1], tile.shape)


def along(tile, row):
    return jnp.broadcast_to(tile[row : row + 1, :], tile.shape)


def newton_step(count, parts, alpha, factor, newton):
    upper, lower = sum_blocks(parts, 0, 2), sum_blocks(parts, 1, 2)
    total = jnp.concatenate([upper, lower[:, 128:HALF]], axis=1)
    packed = jnp.concatenate([total[:, 128 * r : 128 * r + 128] for r in range(16)], axis=0)
    extra = total[:, CORE - 128 : CORE]
    lane, sub = iota2((32, 128), 1), iota2((32, 128), 0)
    s = jnp.concatenate([packed, pltpu.roll(packed, 64, 1)], axis=0)
    top = jnp.where((lane >= sub) & (lane < 64), s, 0.0)
    diagonal = pltpu.roll(jnp.broadcast_to(extra, (32, 128)), 64, 1)
    bottom = jnp.where(
        lane == sub + 32,
        diagonal,
        jnp.where((lane >= 32) & (lane < sub + 32), pltpu.roll(s, 32, 1), 0.0),
    )
    scale = 1.0 / count
    rhs = alpha[...] - 8.0 * extra * scale
    rest = jnp.where(iota2((64, 128), 0) == 0, jnp.broadcast_to(rhs, (64, 128)), 0.0)
    z = jnp.concatenate([top, bottom, rest], axis=0)
    turned = jnp.transpose(z)[0:64]
    lanes, subs = iota2((64, 128), 1), iota2((64, 128), 0)
    both = z[0:64] + jnp.where((lanes == subs) | (lanes >= 64), 0.0, turned)
    a = jnp.where((lanes == subs) | (lanes == subs + 64), 1.0, 0.0) + both * scale
    tiles = [a[8 * t : 8 * t + 8] for t in range(8)]
    right = [across(turned[8 * t : 8 * t + 8], 64) for t in range(8)]
    lane1 = iota2((1, 128), 1)
    solved = jnp.zeros((8, 128), F32)
    for t in range(8):
        base = 8 * t
        columns = [across(tiles[t], base + c) for c in range(8)]
        e = {(i, c): along(columns[c], i) for c in range(8) for i in range(c, 8)}
        line = [along(tiles[t], q) for q in range(8)]
        b = [along(right[t], q) for q in range(8)]
        low, inverse = {}, []
        for c in range(8):
            inverse.append(1.0 / e[c, c])
            for i in range(c + 1, 8):
                low[i, c] = e[i, c] * inverse[c]
            for j in range(c + 1, 8):
                for i in range(j, 8):
                    e[i, j] = e[i, j] - low[i, c] * e[j, c]
            for i in range(c + 1, 8):
                line[i] = line[i] - low[i, c] * line[c]
                b[i] = b[i] - low[i, c] * b[c]
        for i in range(t + 1, 8):
            c_of = []
            for c in range(8):
                value = across(tiles[i], base + c)
                for j in range(c):
                    value = value - c_of[j] * low[c, j]
                c_of.append(value)
            for c in range(8):
                mult = c_of[c] * inverse[c]
                tiles[i] = tiles[i] - mult * line[c]
                right[i] = right[i] - mult * b[c]
        for q in range(8):
            solved = solved + line[q] * (b[q] * inverse[q])
            upper = line[q][0:1] * lax.rsqrt(e[q, q][0:1])
            upper = jnp.where(lane1 >= base + q, upper, 0.0)
            factor[base + q : base + q + 1, :] = upper[:, 0:64]
    newton[...] = pltpu.roll(solved, 64, 1)[0:1, 0:64]


def per_device(perturb, winds, kappa, obs_col, innov, alpha, loc_mask):
    ny = lax.axis_size("y")
    blocks = lax.axis_size(GRID)
    count = float(blocks * 8 * 256)
    sources = (
        perturb.reshape(8, 8, 256),
        winds.reshape(16, 256),
        obs_col,
        innov.reshape(8, 256),
        loc_mask,
    )
    own, near = call(
        pack_block,
        [shape(12, 8, 256), shape(2, 8, 256)],
        *(pltpu.with_memory_space_constraint(a, pltpu.HBM) for a in sources),
        space=pltpu.HBM,
        scratch=[pltpu.VMEM(a.shape, a.dtype) for a in sources]
        + [pltpu.SemaphoreType.DMA((len(sources),))],
    )
    low = lax.ppermute(own, GRID, [(i, (i + 1) % blocks) for i in range(blocks)])
    index = lax.axis_index(GRID)
    joined = (index > 0).astype(F32).reshape(1, 1)
    follows = (index < blocks - 1).astype(F32).reshape(1, 1)
    mine = lax.axis_index("y").reshape(1, 1)
    k = kappa.reshape(1, 1)
    wide = jnp.concatenate([alpha, jnp.zeros((64,), F32)]).reshape(1, 128)
    evolved, binned, column = call(
        tangent,
        [shape(8, 8, 256), shape(8, 256), shape(64, 128)],
        low,
        own,
        near,
        k,
        mine,
        joined,
        wide,
        follows,
    )
    field = lax.all_to_all(evolved, "y", 0, 0, tiled=True)
    (part,) = call(gram_block, [shape(ny, 1, PACK)], field, binned, column)
    parts = lax.all_to_all(part, "y", 0, 0, tiled=True)
    part, window = call(
        first_sum,
        [shape(2 * lax.axis_size("x"), 1, HALF), shape(4, 8, 256)],
        parts,
        own,
    )
    parts = lax.all_to_all(part, ("x", "core"), 0, 0, tiled=True)
    (part,) = call(next_sum, [shape(2 * lax.axis_size("z"), 1, HALF)], parts)
    parts = lax.all_to_all(part, ("z", "core"), 0, 0, tiled=True)
    beyond = lax.ppermute(window, GRID, [((i + 1) % blocks, i) for i in range(blocks)])
    (sens,) = call(
        adjoint, [shape(8, 8, 256)], low, own, window, beyond, k, joined, follows
    )
    final = functools.partial(newton_step, count)
    final.__name__ = "newton_step"
    factor, newton = call(final, [shape(64, 64), shape(1, 64)], parts, wide)
    return factor, newton.reshape(64), sens.reshape(8, 1, 8, 256)


def solution(mesh):
    grid, mem = mesh.devices.shape
    side = int((grid // 2) ** 0.5)
    fine = Mesh(mesh.devices.reshape(side, grid // 2 // side, 2, mem), GRID + ("y",))
    in_specs = (
        P("y", None, GRID, None),
        P(None, None, GRID, None),
        P(),
        P(GRID, None),
        P(None, GRID, None),
        P(),
        P("y", GRID, None),
    )
    out_specs = (P(), P(), P("y", None, GRID, None))
    return jax.shard_map(
        per_device, mesh=fine, in_specs=in_specs, out_specs=out_specs, check_vma=False
    )
```
